32 devices in a mesh: group: 4 (over y, x), inner: 8 (over z, core).
Axes of the slice: x: 2, y: 2, z: 4, core: 2. Of those that a mesh axis runs over, the one named last changes fastest.
Arguments:
- tokens_fwd: bfloat16 [2048, 2048], P(('group', 'inner')), may hold values from -6 to 6
- experts_fwd: int32 [2048, 8], P(('group', 'inner')), may hold values from 0 to 31, all different within a row; in each aligned block of 64 rows (0 to 63, 64 to 127, ...) at most 24 rows name the same one
- scores_fwd: float32 [2048, 8], P(('group', 'inner')), may hold values from 0.05 to 1
- tokens_bwd: bfloat16 [2048, 2048], P(('group', 'inner')), may hold values from -6 to 6
- experts_bwd: int32 [2048, 8], P(('group', 'inner')), may hold values from 0 to 31, all different within a row; in each aligned block of 64 rows (0 to 63, 64 to 127, ...) at most 24 rows name the same one
- scores_bwd: float32 [2048, 8], P(('group', 'inner')), may hold values from 0.05 to 1
- cotangent: bfloat16 [2048, 2048], P(('group', 'inner')), may hold values from -6 to 6
- w_in: bfloat16 [32, 2048, 1536], P(('group', 'inner')), may hold values from -0.125 to 0.125
- w_down: bfloat16 [32, 768, 2048], P(('group', 'inner')), may hold values from -0.21875 to 0.21875
Outputs:
- output_fwd: bfloat16 [2048, 2048], P(('group', 'inner'))
- grad_tokens: bfloat16 [2048, 2048], P(('group', 'inner'))
- grad_w_in: bfloat16 [32, 2048, 1536], P(('group', 'inner'))
- grad_w_down: bfloat16 [32, 768, 2048], P(('group', 'inner'))
The draws below stay inside these ranges and needn't reach their ends.
Inputs may be any that keep to these rules, and one draw needn't show every extreme that they name: `experts_fwd`: each token names 8 different experts; among the tokens of one device at most 24 name any one expert. `experts_bwd`: each token names 8 different experts; among the tokens of one device at most 24 name any one expert.
All inputs are finite; a program needn't handle non-finite values.
Results may differ from the reference program's by a relative error of at most 0.0064.
Values may be sent and summed in bfloat16 or wider, within the bound.
A program may use at most 128 MiB of HBM per device.

```python
import math
import jax
import jax.numpy as jnp
import numpy as np
from jax import lax

D = 2048
FF = 768
TOP = 8
TOK_DEV = 64
EXPERTS = 32
CAP = 24
TOKENS = 2048


def levels(stream_key, dims, cuts, low, top_value):
    factor_of = 1.0
    for dim, parts in cuts:
        heights = jax.random.uniform(jax.random.fold_in(jax.random.fold_in(stream_key, 6), dim), (parts,), jnp.float32, low / len(cuts), top_value / len(cuts))
        factor_of = factor_of * jnp.repeat(jnp.exp(heights), dims[dim] // parts).reshape((-1,) + (1,) * (len(dims) - 1 - dim))
    return factor_of


def shared_out(own_key, own, number, rows, count, top, reach, lean):
    ranking = jax.random.permutation(own_key, count)
    crowded, ordinary = load_shares(count, rows * top, reach, lean, True), load_shares(count, rows * top, reach, lean, False)
    places = jnp.arange(count)

    def named(sizes, turn):
        used = int((sizes > 0).sum())
        fixed = max(1, used // 4)
        moved = fixed + (places - fixed + turn * (used - fixed)) % max(1, count - fixed)
        return jnp.zeros((count,), jnp.int32).at[ranking[jnp.where(places < fixed, places, moved)]].set(jnp.asarray(sizes, jnp.int32))

    sizes = jnp.where(number % 4 == 0, named(crowded, number // 4), named(ordinary, number - number // 4 - 1))
    mixed = jax.random.permutation(jax.random.fold_in(own, 3), count)
    donor, receiver = mixed[0:count // 2 * 2:2], mixed[1:count // 2 * 2:2]
    room = jnp.minimum(sizes[donor] - 1, reach - sizes[receiver]) // 2
    room = jnp.where((donor == ranking[0]) | (receiver == ranking[0]) | (sizes[receiver] == 0), 0, jnp.maximum(room, 0))
    moved = jax.random.randint(jax.random.fold_in(own, 4), (count // 2,), 0, 1 << 20) % (room + 1)
    sizes = sizes.at[donor].add(-moved).at[receiver].add(moved)
    members = jnp.searchsorted(jnp.cumsum(sizes), jnp.arange(rows * top), side="right").astype(jnp.int32)
    table = members.reshape(top, rows).T
    table = table[jax.random.permutation(jax.random.fold_in(own, 1), rows)]
    turn = jax.random.randint(jax.random.fold_in(own, 2), (rows, 1), 0, top)
    return jnp.take_along_axis(table, (jnp.arange(top)[None, :] + turn) % top, axis=1)


def load_shares(amount, total, reach, slope, full):
    loads = [(1 << 20) // math.isqrt(grade ** slope) + 1 for grade in range(1, amount + 1)]
    largest = reach if full else min(reach, max(-(-total // amount), total * loads[0] // sum(loads)))
    least = 1 if total - largest >= amount - 1 else 0
    given, rest = [largest] + [least] * (amount - 1), total - largest - least * (amount - 1)
    while rest > 0:
        free = [i for i in range(1, amount) if given[i] < largest] or [i for i in range(1, amount) if given[i] < reach]
        whole, budget = sum([loads[i] for i in free]), rest
        for i in free:
            addition = min(reach - given[i], max(1, budget * loads[i] // whole), rest)
            given[i] = given[i] + addition
            rest = rest - addition
    return np.array(given)


def scatter_about(stream_key, shape, deviation, limit, shards=(), held_as=jnp.bfloat16):
    result = deviation * jax.random.normal(stream_key, shape, jnp.float32)
    if shards:
        result = result * levels(stream_key, shape, shards, -0.22, 0.18)
    return jnp.clip(result, -limit, limit).astype(held_as)


def setup_inputs(seed: int = 0) -> dict:
    seeds = jax.random.split(jax.random.key(seed), 10)
    tokens_fwd = scatter_about(seeds[0], (TOKENS, D), 1.0, 6.0, ((0, 32),))
    experts_fwd_keys = jax.random.split(jax.random.fold_in(seeds[1], 1), TOKENS // TOK_DEV)
    experts_fwd_turns = jax.random.permutation(jax.random.fold_in(seeds[1], 3), TOKENS // TOK_DEV)
    experts_fwd = jax.vmap(lambda own, number: shared_out(jax.random.fold_in(seeds[1], 2), own, number, TOK_DEV, EXPERTS, TOP, CAP, 2))(experts_fwd_keys, experts_fwd_turns).reshape((TOKENS, TOP))
    scores_fwd = jnp.clip(jnp.exp(math.log(1.0) - 2.9957323 * jax.random.uniform(seeds[2], (TOKENS, TOP), jnp.float32) ** levels(seeds[2], (TOKENS, TOP), ((0, 32),), -0.2, 0.2)), 0.05, 1.0)
    tokens_bwd = scatter_about(seeds[3], (TOKENS, D), 1.0, 6.0, ((0, 32),))
    experts_bwd_keys = jax.random.split(jax.random.fold_in(seeds[4], 1), TOKENS // TOK_DEV)
    experts_bwd_turns = jax.random.permutation(jax.random.fold_in(seeds[4], 3), TOKENS // TOK_DEV)
    experts_bwd = jax.vmap(lambda own, number: shared_out(jax.random.fold_in(seeds[4], 2), own, number, TOK_DEV, EXPERTS, TOP, CAP, 2))(experts_bwd_keys, experts_bwd_turns).reshape((TOKENS, TOP))
    scores_bwd = jnp.clip(jnp.exp(math.log(1.0) - 2.9957323 * jax.random.uniform(seeds[5], (TOKENS, TOP), jnp.float32) ** levels(seeds[5], (TOKENS, TOP), ((0, 32),), -0.2, 0.2)), 0.05, 1.0)
    cotangent = scatter_about(seeds[6], (TOKENS, D), 1.0, 6.0, ((0, 32),))
    w_in = scatter_about(seeds[7], (EXPERTS, D, 2 * FF), D ** -0.5, 0.125, ((0, 32),))
    w_down = scatter_about(seeds[8], (EXPERTS, FF, D), FF ** -0.5, 0.21875, ((0, 32),))
    return {"tokens_fwd": tokens_fwd, "experts_fwd": experts_fwd, "scores_fwd": scores_fwd, "tokens_bwd": tokens_bwd, "experts_bwd": experts_bwd, "scores_bwd": scores_bwd, "cotangent": cotangent, "w_in": w_in, "w_down": w_down}


def expert_forward(tok_rows, w_in_e, w_down_e):
    width = w_down_e.shape[0]
    projected = jnp.dot(tok_rows, w_in_e, preferred_element_type=jnp.float32)
    gate_part = projected[:, :width]
    up_part = projected[:, width:]
    hidden = (gate_part * jax.nn.sigmoid(gate_part) * up_part).astype(jnp.bfloat16)
    return jnp.dot(hidden, w_down_e, preferred_element_type=jnp.float32).astype(jnp.bfloat16)


def expert_backward(tok_rows, cot_rows, w_in_e, w_down_e):
    width = w_down_e.shape[0]
    projected = jnp.dot(tok_rows, w_in_e, preferred_element_type=jnp.float32)
    gate_part = projected[:, :width]
    up_part = projected[:, width:]
    sigmoid_gate = jax.nn.sigmoid(gate_part)
    hidden = (gate_part * sigmoid_gate * up_part).astype(jnp.bfloat16)
    contract_rows = (((0,), (0,)), ((), ()))
    contract_cols = (((1,), (1,)), ((), ()))
    grad_down = lax.dot_general(hidden, cot_rows, contract_rows, preferred_element_type=jnp.float32).astype(jnp.bfloat16)
    d_hidden = lax.dot_general(cot_rows, w_down_e, contract_cols, preferred_element_type=jnp.float32)
    d_gate = d_hidden * up_part * sigmoid_gate * (1.0 + gate_part * (1.0 - sigmoid_gate))
    d_up = d_hidden * gate_part * sigmoid_gate
    d_proj = jnp.concatenate([d_gate, d_up], axis=1).astype(jnp.bfloat16)
    grad_inner = lax.dot_general(tok_rows, d_proj, contract_rows, preferred_element_type=jnp.float32).astype(jnp.bfloat16)
    row_grad = lax.dot_general(d_proj, w_in_e, contract_cols, preferred_element_type=jnp.float32).astype(jnp.bfloat16)
    return row_grad, grad_inner, grad_down


def assignment_tables(expert_ids, scores):
    blocks = TOKENS // TOK_DEV
    flat_ids = expert_ids.reshape(blocks, TOK_DEV * TOP).astype(jnp.int32)
    labels = jnp.arange(EXPERTS, dtype=jnp.int32)
    onehot = (flat_ids[:, :, None] == labels[None, None, :]).astype(jnp.int32)
    before = jnp.cumsum(onehot, axis=1) - onehot
    slot_pos = jnp.sum(before * onehot, axis=2).astype(jnp.int32)
    block_of = jnp.arange(blocks, dtype=jnp.int32)[:, None]
    token_of = block_of * TOK_DEV + jnp.arange(TOK_DEV * TOP, dtype=jnp.int32)[None, :] // TOP
    target = ((flat_ids * blocks + block_of) * CAP + slot_pos).reshape(-1).astype(jnp.int32)
    source = jnp.full((EXPERTS * blocks * CAP,), TOKENS, jnp.int32).at[target].set(token_of.reshape(-1).astype(jnp.int32))
    weights = scores / jnp.sum(scores, axis=1, keepdims=True)
    scaled = jnp.zeros((EXPERTS * blocks * CAP,), jnp.float32).at[target].set(weights.reshape(-1).astype(jnp.float32))
    return source.reshape(EXPERTS, blocks * CAP), scaled.reshape(EXPERTS, blocks * CAP)


def reference(tokens_fwd, experts_fwd, scores_fwd, tokens_bwd, experts_bwd, scores_bwd, cotangent, w_in, w_down):
    source_fwd, scaled_fwd = assignment_tables(experts_fwd, scores_fwd)
    source_bwd, scaled_bwd = assignment_tables(experts_bwd, scores_bwd)
    zero_row = jnp.zeros((1, D), jnp.bfloat16)
    fwd_padded = jnp.concatenate([tokens_fwd, zero_row], axis=0)
    bwd_padded = jnp.concatenate([tokens_bwd, zero_row], axis=0)
    cot_padded = jnp.concatenate([cotangent, zero_row], axis=0)

    def expert_step(totals, inputs):
        out_total, grad_total = totals
        w_in_e, w_down_e, src_f, scl_f, src_b, scl_b = inputs
        expert_out = expert_forward(fwd_padded[src_f], w_in_e, w_down_e)
        out_total = out_total.at[src_f].add(scl_f[:, None] * expert_out.astype(jnp.float32))
        cot_rows = (scl_b[:, None] * cot_padded[src_b].astype(jnp.float32)).astype(jnp.bfloat16)
        row_grad, grad_inner, grad_down = expert_backward(bwd_padded[src_b], cot_rows, w_in_e, w_down_e)
        grad_total = grad_total.at[src_b].add(row_grad.astype(jnp.float32))
        return (out_total, grad_total), (grad_inner, grad_down)

    start = (jnp.zeros((TOKENS + 1, D), jnp.float32), jnp.zeros((TOKENS + 1, D), jnp.float32))
    (out_total, grad_total), (grad_w_in, grad_w_down) = lax.scan(
        expert_step, start, (w_in, w_down, source_fwd, scaled_fwd, source_bwd, scaled_bwd))
    output_fwd = out_total[:TOKENS].astype(jnp.bfloat16)
    grad_tokens = grad_total[:TOKENS].astype(jnp.bfloat16)
    return output_fwd, grad_tokens, grad_w_in, grad_w_down
```

```python
import functools
import math

import jax
import jax.numpy as jnp
from jax import lax
from jax.experimental import pallas as pl
from jax.experimental.pallas import tpu as pltpu
from jax.sharding import PartitionSpec as P

MESH = pl.DeviceIdType.MESH
BF = jnp.bfloat16
F32 = jnp.float32
ROWS = (((0,), (0,)), ((), ()))
COLS = (((1,), (1,)), ((), ()))


def mm(a, b):
    return jnp.dot(a, b, preferred_element_type=F32)


def mm_rows(a, b):
    return lax.dot_general(a, b, ROWS, preferred_element_type=F32)


def mm_cols(a, b):
    return lax.dot_general(a, b, COLS, preferred_element_type=F32)


def tile_of(size, most):
    return max(t for t in range(128, most + 1, 128) if size % t == 0)


def loop(count, body):
    lax.fori_loop(0, count, lambda k, c: (body(k), c)[1], 0)


def layer_kernel(dims, idf_ref, scf_ref, idb_ref, scb_ref, xb_ref, ct_ref, xf_ref, win_hbm, wdn_hbm,
                 of_ref, gt_ref, gin_hbm, gdn_hbm,
                 tab_ref, tabs, win_ref, wdn_ref, rb_ref, rc_ref, rf, hid_ref, dpr_ref,
                 gath, send, parts, near, stage, stage_sem, own_sem, w_sem,
                 tab_s, tab_r, gath_s, gath_r, dense_s, dense_r, disp_s, disp_r,
                 ret_s, ret_r, near_s, near_r, part_s, part_r, free):
    Z, H, L, C, T, J, inner = dims
    D = H * L
    ZP, JC, JT = Z // J, J * C, J * T
    B = H * ZP
    DC = D * JC
    ff, width = wdn_ref.shape
    load_in = pltpu.make_async_copy(win_hbm, win_ref, w_sem.at[0])
    load_down = pltpu.make_async_copy(wdn_hbm, wdn_ref, w_sem.at[1])
    load_in.start()
    load_down.start()
    g = lax.axis_index("group")
    i = lax.axis_index("inner")
    zo, low = i // L, lax.rem(i, L)
    zq, zj = zo // J, lax.rem(zo, J)
    first, second = g // H, lax.rem(g, H)

    def axes_of(l):
        odd = lax.rem(l, 2)
        pack = first * (1 - odd) + second * odd
        dense = second * (1 - odd) + first * odd
        return pack, dense, H - odd * (H - 1), 1 + odd * (H - 1)

    pc, dc, sp, sd = axes_of(low)
    me = pc * L + low
    own = low * H + pc
    A = H * D
    ma = g * L + low

    def plane(a):
        return (a // L, zo * L + lax.rem(a, L))

    def holder(h, z):
        return (pc * sp + lax.rem(dc + h, H) * sd, z * L + low)

    def target(t):
        return ((t // L) * sp + dc * sd, zo * L + lax.rem(t, L))

    barrier = pltpu.get_barrier_semaphore()

    def greet(device):
        pl.semaphore_signal(barrier, inc=1, device_id=device, device_id_type=MESH)

    loop(A - 1, lambda k: greet(plane(lax.rem(ma + k + 1, A))))
    for h in range(H):
        loop(Z - 1, lambda k: greet(holder(h, lax.rem(zo + k + 1, Z))))

    def remote(src, dst, ssem, rsem, device):
        return pltpu.make_async_remote_copy(
            src_ref=src, dst_ref=dst, send_sem=ssem, recv_sem=rsem,
            device_id=device, device_id_type=MESH)

    inputs = (xb_ref, ct_ref, xf_ref)
    recvs = (rb_ref, rc_ref, rf)

    def across(h):
        return (H - h) % H

    def tab_copy(h, k):
        z = lax.rem(zo + k, Z)
        return remote(tab_ref.at[h * Z + z], tabs.at[across(h) * Z + zo],
                      tab_s.at[h, k], tab_r.at[h, k], holder(h, z))

    def gath_copy(s, k):
        z = lax.rem(zo + k, Z)
        return remote(inputs[s], gath.at[s, zo], gath_s.at[s, k], gath_r.at[s, k], holder(0, z))

    def dense_copy(s, h, z):
        return remote(gath.at[s, z], gath.at[s, across(h) * Z + z],
                      dense_s.at[s, h, z], dense_r.at[s, h, z], holder(h, zo))

    for s in range(3):
        gath[s, zo] = inputs[s][...]
    pl.semaphore_wait(barrier, A - 1 + H * (Z - 1))
    for s in range(3):
        for h in range(1, H):
            dense_copy(s, h, zo).start()
        loop(Z - 1, lambda k: gath_copy(s, k + 1).start())

    row = lax.broadcasted_iota(jnp.int32, (H * Z * D, JT), 0)
    h_of, z_of, t_of = row // (Z * D), (row // D) % Z, row % D
    g_of = (t_of // L) * sp + ((dc + h_of) % H) * sd
    expert = (g_of * inner + z_of * L + t_of % L).astype(F32)
    mine = lax.broadcasted_iota(jnp.int32, (1, JT), 1) // T == zj
    earlier = (lax.broadcasted_iota(jnp.int32, (JT, JT), 0)
               < lax.broadcasted_iota(jnp.int32, (JT, JT), 1)).astype(F32).astype(BF)
    tab_ref[...] = jnp.zeros_like(tab_ref)
    for which, (id_ref, sc_ref) in enumerate(((idf_ref, scf_ref), (idb_ref, scb_ref))):
        ids = jnp.where(mine, id_ref[...].astype(F32), -1.0)
        scores = sc_ref[...]
        weights = scores / jnp.sum(scores, axis=0, keepdims=True)
        named = jnp.zeros((H * Z * D, JT), F32)
        weight = jnp.zeros((H * Z * D, JT), F32)
        for k in range(ids.shape[0]):
            hit = jnp.broadcast_to(ids[k:k + 1], (H * Z * D, JT)) == expert
            named = named + hit.astype(F32)
            weight = weight + jnp.where(hit, jnp.broadcast_to(weights[k:k + 1], (H * Z * D, JT)), 0.0)
        slot = jnp.where(named > 0.5, mm(named.astype(BF), earlier), -1.0)
        for b in range(H * Z):
            tab_ref[b, 2 * which * D:(2 * which + 1) * D, :JT] = slot[b * D:(b + 1) * D]
            tab_ref[b, (2 * which + 1) * D:(2 * which + 2) * D, :JT] = weight[b * D:(b + 1) * D]

    loop(Z - 1, lambda k: tab_copy(0, k + 1).start())
    for h in range(1, H):
        loop(Z, lambda k: tab_copy(h, k).start())
    tabs[zo] = tab_ref[zo]

    def hot(b, which):
        slots = [tabs[b * J + j, which * 2 * D:(which * 2 + 1) * D, :JT] for j in range(J)]
        want = lax.broadcasted_iota(jnp.int32, (C, JT), 0).astype(F32)
        return jnp.concatenate(
            [(jnp.broadcast_to(slots[j][t:t + 1], (C, JT)) == want).astype(F32)
             for t in range(D) for j in range(J)], axis=0)

    def weighted(b, which):
        w = [tabs[b * J + j, (which * 2 + 1) * D:(which * 2 + 2) * D, :JT] for j in range(J)]
        spread = jnp.concatenate(
            [jnp.broadcast_to(w[j][t:t + 1], (C, JT)) for t in range(D) for j in range(J)], axis=0)
        full = hot(b, which) * spread
        high = full.astype(BF)
        return high, (full - high.astype(F32)).astype(BF)

    def rows_at(ref, index):
        return ref.at[pl.ds(pl.multiple_of(index * JC, 16), JC)]

    def place(e, b):
        return e * B + b

    def disp_copy(s, b, k):
        t = lax.rem(me + k, D)
        return remote(rows_at(send.at[s], b * D + t), rows_at(recvs[s], place(own, b)),
                      disp_s.at[s, b * D + t], disp_r.at[s, place(own, b)], target(t))

    def disp_in(s, b, k):
        at = place(lax.rem(own + k, D), b)
        return remote(rows_at(send.at[s], 0), rows_at(recvs[s], at),
                      disp_s.at[s, 0], disp_r.at[s, at], target(lax.rem(me + k, D)))

    def own_copy(s, b):
        return pltpu.make_async_copy(
            rows_at(send.at[s], b * D + me), rows_at(recvs[s], place(own, b)), own_sem.at[s, b])

    def span(index, size):
        return pl.ds(pl.multiple_of(index * size, size), size)

    tp = tile_of(width, 512)

    def pack(s, b):
        at = span(b, DC)
        if s == 1:
            picks = weighted(b, 1)
        else:
            picks = (hot(b, 1 if s == 0 else 0).astype(BF),)

        def one(c):
            cols = span(c, tp)
            value = gath[s, pl.ds(b * J, J), :, cols].reshape(JT, tp)
            total = mm(picks[0], value)
            for more in picks[1:]:
                total = total + mm(more, value)
            send[s, at, cols] = total.astype(BF)

        loop(width // tp, one)
        loop(D - 1, lambda k: disp_copy(s, b, k + 1).start())
        own_copy(s, b).start()

    def direct(s, m):
        zp = lax.rem(zq + ZP - m, ZP)
        fixed = isinstance(m, int) and m == 0
        for j in range(1 if fixed else 0, J):
            z = zp * J + lax.rem(zj + j, J)
            k = lax.rem(zo + Z - z, Z)
            gath_copy(s, k).wait_recv()
            for h in range(1, H):
                dense_copy(s, h, z).start()
            if s == 0:
                tab_copy(0, k).wait()
        pack(s, zp)

    def relay(s, m):
        zp = lax.rem(zq + ZP - m, ZP)
        for h in range(1, H):
            for j in range(J):
                z = zp * J + j
                if s == 0:
                    tab_copy(across(h), lax.rem(zo + Z - z, Z)).wait()
                dense_copy(s, across(h), z).wait_recv()
            pack(s, h * ZP + zp)

    for s in range(3):
        direct(s, 0)
        if s > 0:
            relay(s - 1, ZP - 1)

        def step(m, s=s):
            direct(s, m + 1)
            relay(s, m)

        loop(ZP - 1, step)
    relay(2, ZP - 1)

    def arrive(s):
        def one(b):
            loop(D - 1, lambda k: disp_in(s, b, k + 1).wait_recv())
            loop(D - 1, lambda k: disp_copy(s, b, k + 1).wait_send())
            own_copy(s, b).wait()

        loop(B, one)
        if s > 0:
            loop(D - 1, lambda k: pl.semaphore_signal(
                free.at[s - 1], inc=1, device_id=target(lax.rem(me + k + 1, D)), device_id_type=MESH))

    tf = tile_of(ff, 256)
    tw = tile_of(width, 256)
    chunk = A * Z * C // 2
    results = (rf, send.at[0])
    backs = (send.at[2], send.at[1])

    def ret_copy(s, b, k):
        e = lax.rem(own + k, D)
        l = e // H
        p, d, step_p, step_d = axes_of(l)
        at = b * D + p * L + low
        return remote(rows_at(results[s], place(e, b)), rows_at(backs[s], at),
                      ret_s.at[s, place(e, b)], ret_r.at[s, at],
                      (lax.rem(e, H) * step_p + d * step_d, zo * L + l))

    def ret_in(s, b, k):
        t = lax.rem(me + k, D)
        return remote(rows_at(results[s], 0), rows_at(backs[s], b * D + t),
                      ret_s.at[s, 0], ret_r.at[s, b * D + t], target(t))

    def own_back(s, b):
        return pltpu.make_async_copy(
            rows_at(results[s], place(own, b)), rows_at(backs[s], b * D + me), own_sem.at[3 + s, b])

    def give_back(s):
        pl.semaphore_wait(free.at[1 - s], D - 1)

        def one(n):
            b = lax.rem(n // ZP + 1, H) * ZP + lax.rem(zq + lax.rem(n, ZP) + 1, ZP)
            loop(D - 1, lambda k: ret_copy(s, b, k + 1).start())
            own_back(s, b).start()

        loop(B, one)

    arrive(0)
    arrive(1)
    load_in.wait()
    load_down.wait()

    def bwd_rows(r):
        at = span(r, chunk)

        def hidden_tile(j):
            cols = span(j, tf)
            ups = pl.ds(pl.multiple_of(ff + j * tf, 128), tf)
            gate = mm(rb_ref[at], win_ref[:, cols])
            up = mm(rb_ref[at], win_ref[:, ups])
            d_hid = mm_cols(rc_ref[at], wdn_ref[cols])
            sig = jax.nn.sigmoid(gate)
            hid_ref[at, cols] = (gate * sig * up).astype(BF)
            dpr_ref[at, cols] = (d_hid * up * sig * (1.0 + gate * (1.0 - sig))).astype(BF)
            dpr_ref[at, ups] = (d_hid * gate * sig).astype(BF)

        loop(ff // tf, hidden_tile)

        def grad_tile(j):
            cols = span(j, tw)
            results[1][at, cols] = mm_cols(dpr_ref[at], win_ref[cols]).astype(BF)

        loop(width // tw, grad_tile)

    loop(2, bwd_rows)
    give_back(1)

    arrive(2)

    def fwd_rows(r):
        at = span(r, chunk)

        def hidden_tile(j):
            cols = span(j, tf)
            gate = mm(rf[at], win_ref[:, cols])
            up = mm(rf[at], win_ref[:, pl.ds(pl.multiple_of(ff + j * tf, 128), tf)])
            stage[pl.ds(0, chunk), cols] = (gate * jax.nn.sigmoid(gate) * up).astype(BF)

        loop(ff // tf, hidden_tile)

        def out_tile(j):
            cols = span(j, tw)
            rf[at, cols] = mm(stage[pl.ds(0, chunk), pl.ds(0, ff)], wdn_ref[:, cols]).astype(BF)

        loop(width // tw, out_tile)

    loop(2, fwd_rows)
    give_back(0)

    def near_copy(s, h, zp):
        return remote(gath.at[s, pl.ds((h * ZP + zp) * J, J)],
                      near.at[s, pl.ds(((across(h) - 1) * ZP + zp) * J, J)],
                      near_s.at[s, h, zp], near_r.at[s, h, zp], holder(h, zo))

    def gathered(s, b, sides=()):
        loop(D - 1, lambda k: ret_in(s, b, k + 1).wait_recv())
        own_back(s, b).wait()
        for wait, _ in sides:
            wait()
        at = span(b, DC)
        picks = weighted(b, 0) if s == 0 else (hot(b, 1).astype(BF),)

        def one(c):
            cols = span(c, tp)
            value = backs[s][at, cols]
            total = mm_rows(picks[0], value)
            for more in picks[1:]:
                total = total + mm_rows(more, value)
            for _, first in sides:
                total = total + near[s, pl.ds(first, J), :, cols].reshape(JT, tp).astype(F32)
            gath[s, pl.ds(b * J, J), :, cols] = total.astype(BF).reshape(J, T, tp)

        loop(width // tp, one)

    def half_way(s):
        def one(m):
            zp = lax.rem(zq + m + 1, ZP)
            for h in range(1, H):
                gathered(s, h * ZP + zp)
                near_copy(s, h, zp).start()

        loop(ZP, one)

    def part_copy(s, k):
        z = lax.rem(zo + k, Z)
        return remote(gath.at[s, z], parts.at[s, zo], part_s.at[s, k], part_r.at[s, k], holder(0, z))

    def combine(s):
        for h in range(1, H):
            loop(Z, lambda z: dense_copy(s, h, z).wait_send())

        def pair(m):
            zp = lax.rem(zq + m, ZP)
            gathered(s, zp, [(near_copy(s, across(h), zp).wait_recv, ((h - 1) * ZP + zp) * J)
                             for h in range(1, H)])
            fixed = isinstance(m, int) and m == 0
            for j in range(1 if fixed else 0, J):
                part_copy(s, lax.rem(zp * J + lax.rem(zj + j, J) + Z - zo, Z)).start()

        loop(ZP - 1, lambda m: pair(m + 1))
        pair(0)
        parts[s, zo] = gath[s, zo]

    half_way(1)

    tg = math.gcd(tf, tw)
    count_in, count_down = width // tg, ff // tg

    def in_copy(j):
        slot = lax.rem(j, 2)
        return pltpu.make_async_copy(
            stage.at[span(slot, tg), pl.ds(0, 2 * ff)], gin_hbm.at[span(j, tg)], stage_sem.at[slot])

    def down_copy(j):
        slot = lax.rem(j, 2)
        return pltpu.make_async_copy(
            stage.at[span(slot, tg), pl.ds(0, width)], gdn_hbm.at[span(j, tg)], stage_sem.at[slot])

    def in_tile(j):
        value = mm_rows(rb_ref[:, span(j, tg)], dpr_ref[...]).astype(BF)

        @pl.when(j >= 2)
        def _():
            in_copy(j - 2).wait()

        stage[span(lax.rem(j, 2), tg), pl.ds(0, 2 * ff)] = value
        in_copy(j).start()

    loop(count_in, in_tile)
    for j in range(max(0, count_in - 2), count_in):
        in_copy(j).wait()

    combine(1)
    half_way(0)

    def down_tile(j):
        value = mm_rows(hid_ref[:, span(j, tg)], rc_ref[...]).astype(BF)

        @pl.when(j >= 2)
        def _():
            down_copy(j - 2).wait()

        stage[span(lax.rem(j, 2), tg), pl.ds(0, width)] = value
        down_copy(j).start()

    loop(count_down, down_tile)
    for j in range(max(0, count_down - 2), count_down):
        down_copy(j).wait()

    combine(0)
    for s, out in ((1, gt_ref), (0, of_ref)):
        loop(Z - 1, lambda k: part_copy(s, k + 1).wait())
        total = parts[s, 0].astype(F32)
        for z in range(1, Z):
            total = total + parts[s, z].astype(F32)
        out[...] = total.astype(BF)
    for s in range(3):
        loop(Z - 1, lambda k: gath_copy(s, k + 1).wait_send())
    for s in range(2):
        def sent(b, s=s):
            loop(D - 1, lambda k: ret_copy(s, b, k + 1).wait_send())

        loop(B, sent)
        for h in range(1, H):
            loop(ZP, lambda zp: near_copy(s, h, zp).wait_send())
    for h in range(1, H):
        loop(Z, lambda z: dense_copy(2, h, z).wait_send())


def shards(tokens_fwd, experts_fwd, scores_fwd, tokens_bwd, experts_bwd, scores_bwd,
           cotangent, w_in, w_down):
    G, inner = lax.axis_size("group"), lax.axis_size("inner")
    n = G * inner
    T, top = experts_fwd.shape
    width = tokens_fwd.shape[1]
    ff = w_down.shape[1]
    capacity = max(2, 3 * T * top // (2 * n))
    C = -(-capacity // 8) * 8
    Z = max(d for d in range(1, inner + 1) if inner % d == 0 and d * d <= n)
    L = inner // Z
    H = math.isqrt(G)
    assert H * H == G
    D = H * L
    rows = n * C
    J = 2
    assert Z % J == 0
    lanes = -(-J * T // 128) * 128
    vmem = pl.BlockSpec(memory_space=pltpu.VMEM)
    dma = pltpu.SemaphoreType.DMA
    hbm = pl.BlockSpec(memory_space=pl.ANY)
    tg = math.gcd(tile_of(ff, 256), tile_of(width, 256))
    out_fwd, grad_tok, grad_in, grad_down = pl.pallas_call(
        functools.partial(layer_kernel, (Z, H, L, C, T, J, inner)),
        out_shape=(
            jax.ShapeDtypeStruct((T, width), BF),
            jax.ShapeDtypeStruct((T, width), BF),
            jax.ShapeDtypeStruct((width, 2 * ff), BF),
            jax.ShapeDtypeStruct((ff, width), BF),
        ),
        in_specs=[vmem] * 7 + [hbm] * 2,
        out_specs=(vmem, vmem, hbm, hbm),
        scratch_shapes=[
            pltpu.VMEM((H * Z, 4 * D, lanes), F32),
            pltpu.VMEM((H * Z, 4 * D, lanes), F32),
            pltpu.VMEM((width, 2 * ff), BF),
            pltpu.VMEM((ff, width), BF),
            pltpu.VMEM((rows, width), BF),
            pltpu.VMEM((rows, width), BF),
            pltpu.VMEM((rows, width), BF),
            pltpu.VMEM((rows, ff), BF),
            pltpu.VMEM((rows, 2 * ff), BF),
            pltpu.VMEM((3, H * Z, T, width), BF),
            pltpu.VMEM((3, rows, width), BF),
            pltpu.VMEM((2, Z, T, width), BF),
            pltpu.VMEM((2, (H - 1) * Z, T, width), BF),
            pltpu.VMEM((max(2 * tg, rows // 2), max(2 * ff, width)), BF),
            dma((2,)),
            dma((5, H * Z)), dma((2,)), dma((H, Z)), dma((H, Z)), dma((3, Z)), dma((3, Z)),
            dma((3, H, Z)), dma((3, H, Z)), dma((3, n)), dma((3, n)),
            dma((2, n)), dma((2, n)), dma((2, H, Z)), dma((2, H, Z)), dma((2, Z)), dma((2, Z)),
            pltpu.SemaphoreType.REGULAR((2,)),
        ],
        compiler_params=pltpu.CompilerParams(
            collective_id=0, has_side_effects=True, vmem_limit_bytes=67043328),
        name="moe_layer",
    )(*(jnp.concatenate([a.T] * J, axis=1) for a in (experts_fwd, scores_fwd, experts_bwd, scores_bwd)),
      tokens_bwd, cotangent, tokens_fwd, w_in[0], w_down[0])
    return out_fwd, grad_tok, grad_in[None], grad_down[None]


def solution(mesh):
    two, three = P(("group", "inner"), None), P(("group", "inner"), None, None)
    return jax.shard_map(
        shards, mesh=mesh,
        in_specs=(two,) * 7 + (three,) * 2,
        out_specs=(two, two, three, three),
        check_vma=False,
    )
```

```python
import functools
import math

import jax
import jax.numpy as jnp
from jax import lax
from jax.experimental import pallas as pl
from jax.experimental.pallas import tpu as pltpu
from jax.sharding import PartitionSpec as P

MESH = pl.DeviceIdType.MESH
BF = jnp.bfloat16
F32 = jnp.float32
ROWS = (((0,), (0,)), ((), ()))
COLS = (((1,), (1,)), ((), ()))


def mm(a, b):
    return jnp.dot(a, b, preferred_element_type=F32)


def mm_rows(a, b):
    return lax.dot_general(a, b, ROWS, preferred_element_type=F32)


def mm_cols(a, b):
    return lax.dot_general(a, b, COLS, preferred_element_type=F32)


def tile_of(size, most):
    return max(t for t in range(128, most + 1, 128) if size % t == 0)


def loop(count, body):
    lax.fori_loop(0, count, lambda k, c: (body(k), c)[1], 0)


def layer_kernel(dims, idf_ref, scf_ref, idb_ref, scb_ref, xb_ref, ct_ref, xf_ref, win_hbm, wdn_hbm,
                 of_ref, gt_ref, gin_hbm, gdn_hbm,
                 tab_ref, tabs, win_ref, wdn_ref, rb_ref, rc_ref, rf, hid_ref, dpr_ref,
                 gath, send, parts, near, stage, stage_sem, own_sem, w_sem,
                 tab_s, tab_r, gath_s, gath_r, dense_s, dense_r, disp_s, disp_r,
                 ret_s, ret_r, near_s, near_r, part_s, part_r, free):
    Z, H, L, C, T, J, inner = dims
    D = H * L
    ZP, JC, JT = Z // J, J * C, J * T
    B = H * ZP
    DC = D * JC
    ff, width = wdn_ref.shape
    load_in = pltpu.make_async_copy(win_hbm, win_ref, w_sem.at[0])
    load_down = pltpu.make_async_copy(wdn_hbm, wdn_ref, w_sem.at[1])
    load_in.start()
    load_down.start()
    g = lax.axis_index("group")
    i = lax.axis_index("inner")
    zo, low = i // L, lax.rem(i, L)
    zq, zj = zo // J, lax.rem(zo, J)
    first, second = g // H, lax.rem(g, H)

    def axes_of(l):
        odd = lax.rem(l, 2)
        pack = first * (1 - odd) + second * odd
        dense = second * (1 - odd) + first * odd
        return pack, dense, H - odd * (H - 1), 1 + odd * (H - 1)

    pc, dc, sp, sd = axes_of(low)
    me = pc * L + low
    own = low * H + pc
    A = H * D
    ma = g * L + low

    def plane(a):
        return (a // L, zo * L + lax.rem(a, L))

    def holder(h, z):
        return (pc * sp + lax.rem(dc + h, H) * sd, z * L + low)

    def target(t):
        return ((t // L) * sp + dc * sd, zo * L + lax.rem(t, L))

    barrier = pltpu.get_barrier_semaphore()

    def greet(device):
        pl.semaphore_signal(barrier, inc=1, device_id=device, device_id_type=MESH)

    loop(A - 1, lambda k: greet(plane(lax.rem(ma + k + 1, A))))
    for h in range(H):
        loop(Z - 1, lambda k: greet(holder(h, lax.rem(zo + k + 1, Z))))

    def remote(src, dst, ssem, rsem, device):
        return pltpu.make_async_remote_copy(
            src_ref=src, dst_ref=dst, send_sem=ssem, recv_sem=rsem,
            device_id=device, device_id_type=MESH)

    inputs = (xb_ref, ct_ref, xf_ref)
    recvs = (rb_ref, rc_ref, rf)

    def across(h):
        return (H - h) % H

    def tab_copy(h, k):
        z = lax.rem(zo + k, Z)
        return remote(tab_ref.at[h * Z + z], tabs.at[across(h) * Z + zo],
                      tab_s.at[h, k], tab_r.at[h, k], holder(h, z))

    def line_copy(s, side, r):
        z = zo - r if side else zo + r
        return remote(gath.at[s, z], gath.at[s, z], gath_s.at[s, side, r], gath_r.at[s, z],
                      holder(0, zo + 1 if side else zo - 1))

    def along(s, r, act):
        @pl.when((zo + 1 < Z) & (zo - r >= 0))
        def _():
            act(line_copy(s, 1, r))

        @pl.when((zo >= 1) & (zo + r < Z))
        def _():
            act(line_copy(s, 0, r))

    def dense_copy(s, h, z):
        return remote(gath.at[s, z], gath.at[s, across(h) * Z + z],
                      dense_s.at[s, h, z], dense_r.at[s, h, z], holder(h, zo))

    for s in range(3):
        gath[s, zo] = inputs[s][...]
    pl.semaphore_wait(barrier, A - 1 + H * (Z - 1))
    for s in range(3):
        for h in range(1, H):
            dense_copy(s, h, zo).start()
    along(0, 0, lambda copy: copy.start())

    row = lax.broadcasted_iota(jnp.int32, (H * Z * D, JT), 0)
    h_of, z_of, t_of = row // (Z * D), (row // D) % Z, row % D
    g_of = (t_of // L) * sp + ((dc + h_of) % H) * sd
    expert = (g_of * inner + z_of * L + t_of % L).astype(F32)
    mine = lax.broadcasted_iota(jnp.int32, (1, JT), 1) // T == zj
    earlier = (lax.broadcasted_iota(jnp.int32, (JT, JT), 0)
               < lax.broadcasted_iota(jnp.int32, (JT, JT), 1)).astype(F32).astype(BF)
    tab_ref[...] = jnp.zeros_like(tab_ref)
    for which, (id_ref, sc_ref) in enumerate(((idf_ref, scf_ref), (idb_ref, scb_ref))):
        ids = jnp.where(mine, id_ref[...].astype(F32), -1.0)
        scores = sc_ref[...]
        weights = scores / jnp.sum(scores, axis=0, keepdims=True)
        named = jnp.zeros((H * Z * D, JT), F32)
        weight = jnp.zeros((H * Z * D, JT), F32)
        for k in range(ids.shape[0]):
            hit = jnp.broadcast_to(ids[k:k + 1], (H * Z * D, JT)) == expert
            named = named + hit.astype(F32)
            weight = weight + jnp.where(hit, jnp.broadcast_to(weights[k:k + 1], (H * Z * D, JT)), 0.0)
        slot = jnp.where(named > 0.5, mm(named.astype(BF), earlier), -1.0)
        for b in range(H * Z):
            tab_ref[b, 2 * which * D:(2 * which + 1) * D, :JT] = slot[b * D:(b + 1) * D]
            tab_ref[b, (2 * which + 1) * D:(2 * which + 2) * D, :JT] = weight[b * D:(b + 1) * D]

    loop(Z - 1, lambda k: tab_copy(0, k + 1).start())
    for h in range(1, H):
        loop(Z, lambda k: tab_copy(h, k).start())
    tabs[zo] = tab_ref[zo]

    def hot(b, which):
        slots = [tabs[b * J + j, which * 2 * D:(which * 2 + 1) * D, :JT] for j in range(J)]
        want = lax.broadcasted_iota(jnp.int32, (C, JT), 0).astype(F32)
        return jnp.concatenate(
            [(jnp.broadcast_to(slots[j][t:t + 1], (C, JT)) == want).astype(F32)
             for t in range(D) for j in range(J)], axis=0)

    def weighted(b, which):
        w = [tabs[b * J + j, (which * 2 + 1) * D:(which * 2 + 2) * D, :JT] for j in range(J)]
        spread = jnp.concatenate(
            [jnp.broadcast_to(w[j][t:t + 1], (C, JT)) for t in range(D) for j in range(J)], axis=0)
        full = hot(b, which) * spread
        high = full.astype(BF)
        return high, (full - high.astype(F32)).astype(BF)

    def rows_at(ref, index):
        return ref.at[pl.ds(pl.multiple_of(index * JC, 16), JC)]

    def place(e, b):
        return e * B + b

    def disp_copy(s, b, k):
        t = lax.rem(me + k, D)
        return remote(rows_at(send.at[s], b * D + t), rows_at(recvs[s], place(own, b)),
                      disp_s.at[s, b * D + t], disp_r.at[s, place(own, b)], target(t))

    def disp_in(s, b, k):
        at = place(lax.rem(own + k, D), b)
        return remote(rows_at(send.at[s], 0), rows_at(recvs[s], at),
                      disp_s.at[s, 0], disp_r.at[s, at], target(lax.rem(me + k, D)))

    def own_copy(s, b):
        return pltpu.make_async_copy(
            rows_at(send.at[s], b * D + me), rows_at(recvs[s], place(own, b)), own_sem.at[s, b])

    def span(index, size):
        return pl.ds(pl.multiple_of(index * size, size), size)

    tp = tile_of(width, 512)

    def pack(s, b):
        at = span(b, DC)
        if s == 1:
            picks = weighted(b, 1)
        else:
            picks = (hot(b, 1 if s == 0 else 0).astype(BF),)

        def one(c):
            cols = span(c, tp)
            value = gath[s, pl.ds(b * J, J), :, cols].reshape(JT, tp)
            total = mm(picks[0], value)
            for more in picks[1:]:
                total = total + mm(more, value)
            send[s, at, cols] = total.astype(BF)

        loop(width // tp, one)
        loop(D - 1, lambda k: disp_copy(s, b, k + 1).start())
        own_copy(s, b).start()

    def landed(s, r):
        for side in range(2):
            @pl.when((zo - r >= 0) if side else (zo + r < Z))
            def _():
                z = zo - r if side else zo + r
                line_copy(s, side, r).wait_recv()
                for h in range(1, H):
                    dense_copy(s, h, z).start()
                if s == 0:
                    tab_copy(0, lax.rem(zo + Z - z, Z)).wait()

        along(s, r, lambda copy: copy.start())

    def direct(s, m):
        pack(s, lax.rem(zq + ZP - m, ZP))

    def relay(s, m):
        zp = lax.rem(zq + ZP - m, ZP)
        for h in range(1, H):
            for j in range(J):
                z = zp * J + j
                if s == 0:
                    tab_copy(across(h), lax.rem(zo + Z - z, Z)).wait()
                dense_copy(s, across(h), z).wait_recv()
            pack(s, h * ZP + zp)

    for s in range(3):
        landed(s, 1)
        if s < 2:
            along(s + 1, 0, lambda copy: copy.start())
        direct(s, 0)
        if s > 0:
            loop(ZP - 1, lambda m: relay(s - 1, m + 1))
        landed(s, 2)
        relay(s, 0)
        for r in range(3, Z):
            landed(s, r)
        loop(ZP - 1, lambda m: direct(s, m + 1))
    loop(ZP - 1, lambda m: relay(2, m + 1))

    def arrive(s):
        def one(b):
            loop(D - 1, lambda k: disp_in(s, b, k + 1).wait_recv())
            loop(D - 1, lambda k: disp_copy(s, b, k + 1).wait_send())
            own_copy(s, b).wait()

        loop(B, one)
        if s > 0:
            loop(D - 1, lambda k: pl.semaphore_signal(
                free.at[s - 1], inc=1, device_id=target(lax.rem(me + k + 1, D)), device_id_type=MESH))

    tf = tile_of(ff, 256)
    tw = tile_of(width, 256)
    chunk = A * Z * C // 2
    results = (rf, send.at[0])
    backs = (send.at[2], send.at[1])

    def ret_copy(s, b, k):
        e = lax.rem(own + k, D)
        l = e // H
        p, d, step_p, step_d = axes_of(l)
        at = b * D + p * L + low
        return remote(rows_at(results[s], place(e, b)), rows_at(backs[s], at),
                      ret_s.at[s, place(e, b)], ret_r.at[s, at],
                      (lax.rem(e, H) * step_p + d * step_d, zo * L + l))

    def ret_in(s, b, k):
        t = lax.rem(me + k, D)
        return remote(rows_at(results[s], 0), rows_at(backs[s], b * D + t),
                      ret_s.at[s, 0], ret_r.at[s, b * D + t], target(t))

    def own_back(s, b):
        return pltpu.make_async_copy(
            rows_at(results[s], place(own, b)), rows_at(backs[s], b * D + me), own_sem.at[3 + s, b])

    def give_back(s):
        pl.semaphore_wait(free.at[1 - s], D - 1)

        def one(n):
            b = lax.rem(n // ZP + 1, H) * ZP + lax.rem(zq + lax.rem(n, ZP) + 1, ZP)
            loop(D - 1, lambda k: ret_copy(s, b, k + 1).start())
            own_back(s, b).start()

        loop(B, one)

    arrive(0)
    arrive(1)
    load_in.wait()
    load_down.wait()

    def bwd_rows(r):
        at = span(r, chunk)

        def hidden_tile(j):
            cols = span(j, tf)
            ups = pl.ds(pl.multiple_of(ff + j * tf, 128), tf)
            gate = mm(rb_ref[at], win_ref[:, cols])
            up = mm(rb_ref[at], win_ref[:, ups])
            d_hid = mm_cols(rc_ref[at], wdn_ref[cols])
            sig = jax.nn.sigmoid(gate)
            hid_ref[at, cols] = (gate * sig * up).astype(BF)
            dpr_ref[at, cols] = (d_hid * up * sig * (1.0 + gate * (1.0 - sig))).astype(BF)
            dpr_ref[at, ups] = (d_hid * gate * sig).astype(BF)

        loop(ff // tf, hidden_tile)

        def grad_tile(j):
            cols = span(j, tw)
            results[1][at, cols] = mm_cols(dpr_ref[at], win_ref[cols]).astype(BF)

        loop(width // tw, grad_tile)

    loop(2, bwd_rows)
    give_back(1)

    arrive(2)

    def fwd_rows(r):
        at = span(r, chunk)

        def hidden_tile(j):
            cols = span(j, tf)
            gate = mm(rf[at], win_ref[:, cols])
            up = mm(rf[at], win_ref[:, pl.ds(pl.multiple_of(ff + j * tf, 128), tf)])
            stage[pl.ds(0, chunk), cols] = (gate * jax.nn.sigmoid(gate) * up).astype(BF)

        loop(ff // tf, hidden_tile)

        def out_tile(j):
            cols = span(j, tw)
            rf[at, cols] = mm(stage[pl.ds(0, chunk), pl.ds(0, ff)], wdn_ref[:, cols]).astype(BF)

        loop(width // tw, out_tile)

    loop(2, fwd_rows)
    give_back(0)

    def near_copy(s, h, zp):
        return remote(gath.at[s, pl.ds((h * ZP + zp) * J, J)],
                      near.at[s, pl.ds(((across(h) - 1) * ZP + zp) * J, J)],
                      near_s.at[s, h, zp], near_r.at[s, h, zp], holder(h, zo))

    def gathered(s, b, sides=()):
        loop(D - 1, lambda k: ret_in(s, b, k + 1).wait_recv())
        own_back(s, b).wait()
        for wait, _ in sides:
            wait()
        at = span(b, DC)
        picks = weighted(b, 0) if s == 0 else (hot(b, 1).astype(BF),)

        def one(c):
            cols = span(c, tp)
            value = backs[s][at, cols]
            total = mm_rows(picks[0], value)
            for more in picks[1:]:
                total = total + mm_rows(more, value)
            for _, first in sides:
                total = total + near[s, pl.ds(first, J), :, cols].reshape(JT, tp).astype(F32)
            gath[s, pl.ds(b * J, J), :, cols] = total.astype(BF).reshape(J, T, tp)

        loop(width // tp, one)

    def half_way(s):
        def one(m):
            zp = lax.rem(zq + m + 1, ZP)
            for h in range(1, H):
                gathered(s, h * ZP + zp)
                near_copy(s, h, zp).start()

        loop(ZP, one)

    def part_copy(s, k):
        z = lax.rem(zo + k, Z)
        return remote(gath.at[s, z], parts.at[s, zo], part_s.at[s, k], part_r.at[s, k], holder(0, z))

    def combine(s):
        for h in range(1, H):
            loop(Z, lambda z: dense_copy(s, h, z).wait_send())
        for r in range(Z - 1):
            along(s, r, lambda copy: copy.wait_send())

        def pair(m):
            zp = lax.rem(zq + m, ZP)
            gathered(s, zp, [(near_copy(s, across(h), zp).wait_recv, ((h - 1) * ZP + zp) * J)
                             for h in range(1, H)])
            fixed = isinstance(m, int) and m == 0
            for j in range(1 if fixed else 0, J):
                part_copy(s, lax.rem(zp * J + lax.rem(zj + j, J) + Z - zo, Z)).start()

        loop(ZP - 1, lambda m: pair(m + 1))
        pair(0)
        parts[s, zo] = gath[s, zo]

    half_way(1)

    tg = math.gcd(tf, tw)
    count_in, count_down = width // tg, ff // tg

    def in_copy(j):
        slot = lax.rem(j, 2)
        return pltpu.make_async_copy(
            stage.at[span(slot, tg), pl.ds(0, 2 * ff)], gin_hbm.at[span(j, tg)], stage_sem.at[slot])

    def down_copy(j):
        slot = lax.rem(j, 2)
        return pltpu.make_async_copy(
            stage.at[span(slot, tg), pl.ds(0, width)], gdn_hbm.at[span(j, tg)], stage_sem.at[slot])

    def in_tile(j):
        value = mm_rows(rb_ref[:, span(j, tg)], dpr_ref[...]).astype(BF)

        @pl.when(j >= 2)
        def _():
            in_copy(j - 2).wait()

        stage[span(lax.rem(j, 2), tg), pl.ds(0, 2 * ff)] = value
        in_copy(j).start()

    loop(count_in, in_tile)
    for j in range(max(0, count_in - 2), count_in):
        in_copy(j).wait()

    combine(1)
    half_way(0)

    def down_tile(j):
        value = mm_rows(hid_ref[:, span(j, tg)], rc_ref[...]).astype(BF)

        @pl.when(j >= 2)
        def _():
            down_copy(j - 2).wait()

        stage[span(lax.rem(j, 2), tg), pl.ds(0, width)] = value
        down_copy(j).start()

    loop(count_down, down_tile)
    for j in range(max(0, count_down - 2), count_down):
        down_copy(j).wait()

    combine(0)
    for s, out in ((1, gt_ref), (0, of_ref)):
        loop(Z - 1, lambda k: part_copy(s, k + 1).wait())
        total = parts[s, 0].astype(F32)
        for z in range(1, Z):
            total = total + parts[s, z].astype(F32)
        out[...] = total.astype(BF)
    for r in range(Z - 1):
        along(2, r, lambda copy: copy.wait_send())
    for s in range(2):
        def sent(b, s=s):
            loop(D - 1, lambda k: ret_copy(s, b, k + 1).wait_send())

        loop(B, sent)
        for h in range(1, H):
            loop(ZP, lambda zp: near_copy(s, h, zp).wait_send())
    for h in range(1, H):
        loop(Z, lambda z: dense_copy(2, h, z).wait_send())


def shards(tokens_fwd, experts_fwd, scores_fwd, tokens_bwd, experts_bwd, scores_bwd,
           cotangent, w_in, w_down):
    G, inner = lax.axis_size("group"), lax.axis_size("inner")
    n = G * inner
    T, top = experts_fwd.shape
    width = tokens_fwd.shape[1]
    ff = w_down.shape[1]
    capacity = max(2, 3 * T * top // (2 * n))
    C = -(-capacity // 8) * 8
    Z = max(d for d in range(1, inner + 1) if inner % d == 0 and d * d <= n)
    L = inner // Z
    H = math.isqrt(G)
    assert H * H == G
    D = H * L
    rows = n * C
    J = 2
    assert Z % J == 0
    lanes = -(-J * T // 128) * 128
    vmem = pl.BlockSpec(memory_space=pltpu.VMEM)
    dma = pltpu.SemaphoreType.DMA
    hbm = pl.BlockSpec(memory_space=pl.ANY)
    tg = math.gcd(tile_of(ff, 256), tile_of(width, 256))
    out_fwd, grad_tok, grad_in, grad_down = pl.pallas_call(
        functools.partial(layer_kernel, (Z, H, L, C, T, J, inner)),
        out_shape=(
            jax.ShapeDtypeStruct((T, width), BF),
            jax.ShapeDtypeStruct((T, width), BF),
            jax.ShapeDtypeStruct((width, 2 * ff), BF),
            jax.ShapeDtypeStruct((ff, width), BF),
        ),
        in_specs=[vmem] * 7 + [hbm] * 2,
        out_specs=(vmem, vmem, hbm, hbm),
        scratch_shapes=[
            pltpu.VMEM((H * Z, 4 * D, lanes), F32),
            pltpu.VMEM((H * Z, 4 * D, lanes), F32),
            pltpu.VMEM((width, 2 * ff), BF),
            pltpu.VMEM((ff, width), BF),
            pltpu.VMEM((rows, width), BF),
            pltpu.VMEM((rows, width), BF),
            pltpu.VMEM((rows, width), BF),
            pltpu.VMEM((rows, ff), BF),
            pltpu.VMEM((rows, 2 * ff), BF),
            pltpu.VMEM((3, H * Z, T, width), BF),
            pltpu.VMEM((3, rows, width), BF),
            pltpu.VMEM((2, Z, T, width), BF),
            pltpu.VMEM((2, (H - 1) * Z, T, width), BF),
            pltpu.VMEM((max(2 * tg, rows // 2), max(2 * ff, width)), BF),
            dma((2,)),
            dma((5, H * Z)), dma((2,)), dma((H, Z)), dma((H, Z)), dma((3, 2, Z)), dma((3, Z)),
            dma((3, H, Z)), dma((3, H, Z)), dma((3, n)), dma((3, n)),
            dma((2, n)), dma((2, n)), dma((2, H, Z)), dma((2, H, Z)), dma((2, Z)), dma((2, Z)),
            pltpu.SemaphoreType.REGULAR((2,)),
        ],
        compiler_params=pltpu.CompilerParams(
            collective_id=0, has_side_effects=True, vmem_limit_bytes=67043328),
        name="moe_layer",
    )(*(jnp.concatenate([a.T] * J, axis=1) for a in (experts_fwd, scores_fwd, experts_bwd, scores_bwd)),
      tokens_bwd, cotangent, tokens_fwd, w_in[0], w_down[0])
    return out_fwd, grad_tok, grad_in[None], grad_down[None]


def solution(mesh):
    two, three = P(("group", "inner"), None), P(("group", "inner"), None, None)
    return jax.shard_map(
        shards, mesh=mesh,
        in_specs=(two,) * 7 + (three,) * 2,
        out_specs=(two, two, three, three),
        check_vma=False,
    )
```

```python
import functools
import math

import jax
import jax.numpy as jnp
from jax import lax
from jax.experimental import pallas as pl
from jax.experimental.pallas import tpu as pltpu
from jax.sharding import PartitionSpec as P

MESH = pl.DeviceIdType.MESH
BF = jnp.bfloat16
F32 = jnp.float32
PIECES = 8
ROWS = (((0,), (0,)), ((), ()))
COLS = (((1,), (1,)), ((), ()))


def mm(a, b):
    return jnp.dot(a, b, preferred_element_type=F32)


def mm_rows(a, b):
    return lax.dot_general(a, b, ROWS, preferred_element_type=F32)


def mm_cols(a, b):
    return lax.dot_general(a, b, COLS, preferred_element_type=F32)


def tile_of(size, most):
    return max(t for t in range(128, most + 1, 128) if size % t == 0)


def loop(count, body):
    lax.fori_loop(0, count, lambda k, c: (body(k), c)[1], 0)


def layer_kernel(dims, idf_ref, scf_ref, idb_ref, scb_ref, xb_ref, ct_ref, xf_ref, win_hbm, wdn_hbm,
                 of_ref, gt_ref, gin_hbm, gdn_hbm,
                 tab_ref, tabs, win_ref, wdn_ref, rb_ref, rc_ref, rf, hid_ref, dpr_ref,
                 gath, send, parts, near, stage, stage_sem, own_sem, w_sem,
                 tab_s, tab_r, gath_s, gath_r, dense_s, dense_r, disp_s, disp_r,
                 ret_s, ret_r, near_s, near_r, part_s, part_r, free):
    Z, H, L, C, T, J, inner = dims
    D = H * L
    ZP, JC, JT = Z // J, J * C, J * T
    B = H * ZP
    DC = D * JC
    ff, width = wdn_ref.shape
    load_in = pltpu.make_async_copy(win_hbm, win_ref, w_sem.at[0])
    load_down = pltpu.make_async_copy(wdn_hbm, wdn_ref, w_sem.at[1])
    load_in.start()
    load_down.start()
    g = lax.axis_index("group")
    i = lax.axis_index("inner")
    zo, low = i // L, lax.rem(i, L)
    zq, zj = zo // J, lax.rem(zo, J)
    first, second = g // H, lax.rem(g, H)

    def axes_of(l):
        odd = lax.rem(l, 2)
        pack = first * (1 - odd) + second * odd
        dense = second * (1 - odd) + first * odd
        return pack, dense, H - odd * (H - 1), 1 + odd * (H - 1)

    pc, dc, sp, sd = axes_of(low)
    me = pc * L + low
    own = low * H + pc
    A = H * D
    ma = g * L + low

    def plane(a):
        return (a // L, zo * L + lax.rem(a, L))

    def holder(h, z):
        return (pc * sp + lax.rem(dc + h, H) * sd, z * L + low)

    def target(t):
        return ((t // L) * sp + dc * sd, zo * L + lax.rem(t, L))

    barrier = pltpu.get_barrier_semaphore()

    def greet(device):
        pl.semaphore_signal(barrier, inc=1, device_id=device, device_id_type=MESH)

    loop(A - 1, lambda k: greet(plane(lax.rem(ma + k + 1, A))))
    for h in range(H):
        loop(Z - 1, lambda k: greet(holder(h, lax.rem(zo + k + 1, Z))))

    def remote(src, dst, ssem, rsem, device):
        return pltpu.make_async_remote_copy(
            src_ref=src, dst_ref=dst, send_sem=ssem, recv_sem=rsem,
            device_id=device, device_id_type=MESH)

    inputs = (xb_ref, ct_ref, xf_ref)
    recvs = (rb_ref, rc_ref, rf)

    def across(h):
        return (H - h) % H

    def tab_copy(h, k):
        z = lax.rem(zo + k, Z)
        return remote(tab_ref.at[h * Z + z], tabs.at[across(h) * Z + zo],
                      tab_s.at[h, k], tab_r.at[h, k], holder(h, z))

    def line_copy(s, side, r):
        z = zo - r if side else zo + r
        return remote(gath.at[s, z], gath.at[s, z], gath_s.at[s, side, r], gath_r.at[s, z],
                      holder(0, zo + 1 if side else zo - 1))

    def along(s, r, act):
        @pl.when((zo + 1 < Z) & (zo - r >= 0))
        def _():
            act(line_copy(s, 1, r))

        @pl.when((zo >= 1) & (zo + r < Z))
        def _():
            act(line_copy(s, 0, r))

    def dense_copy(s, h, z):
        return remote(gath.at[s, z], gath.at[s, across(h) * Z + z],
                      dense_s.at[s, h, z], dense_r.at[s, h, z], holder(h, zo))

    for s in range(3):
        gath[s, zo] = inputs[s][...]
    pl.semaphore_wait(barrier, A - 1 + H * (Z - 1))
    for s in range(3):
        for h in range(1, H):
            dense_copy(s, h, zo).start()
    along(0, 0, lambda copy: copy.start())

    row = lax.broadcasted_iota(jnp.int32, (H * Z * D, JT), 0)
    h_of, z_of, t_of = row // (Z * D), (row // D) % Z, row % D
    g_of = (t_of // L) * sp + ((dc + h_of) % H) * sd
    expert = (g_of * inner + z_of * L + t_of % L).astype(F32)
    mine = lax.broadcasted_iota(jnp.int32, (1, JT), 1) // T == zj
    earlier = (lax.broadcasted_iota(jnp.int32, (JT, JT), 0)
               < lax.broadcasted_iota(jnp.int32, (JT, JT), 1)).astype(F32).astype(BF)
    tab_ref[...] = jnp.zeros_like(tab_ref)
    for which, (id_ref, sc_ref) in enumerate(((idf_ref, scf_ref), (idb_ref, scb_ref))):
        ids = jnp.where(mine, jnp.concatenate([id_ref[...].astype(F32)] * J, axis=1), -1.0)
        scores = jnp.concatenate([sc_ref[...]] * J, axis=1)
        weights = scores / jnp.sum(scores, axis=0, keepdims=True)
        named = jnp.zeros((H * Z * D, JT), F32)
        weight = jnp.zeros((H * Z * D, JT), F32)
        for k in range(ids.shape[0]):
            hit = jnp.broadcast_to(ids[k:k + 1], (H * Z * D, JT)) == expert
            named = named + hit.astype(F32)
            weight = weight + jnp.where(hit, jnp.broadcast_to(weights[k:k + 1], (H * Z * D, JT)), 0.0)
        slot = jnp.where(named > 0.5, mm(named.astype(BF), earlier), -1.0)
        for b in range(H * Z):
            tab_ref[b, 2 * which * D:(2 * which + 1) * D, :JT] = slot[b * D:(b + 1) * D]
            tab_ref[b, (2 * which + 1) * D:(2 * which + 2) * D, :JT] = weight[b * D:(b + 1) * D]

    loop(Z - 1, lambda k: tab_copy(0, k + 1).start())
    for h in range(1, H):
        loop(Z, lambda k: tab_copy(h, k).start())
    tabs[zo] = tab_ref[zo]

    def hot(b, which):
        slots = [tabs[b * J + j, which * 2 * D:(which * 2 + 1) * D, :JT] for j in range(J)]
        want = lax.broadcasted_iota(jnp.int32, (C, JT), 0).astype(F32)
        return jnp.concatenate(
            [(jnp.broadcast_to(slots[j][t:t + 1], (C, JT)) == want).astype(F32)
             for t in range(D) for j in range(J)], axis=0)

    def weighted(b, which):
        w = [tabs[b * J + j, (which * 2 + 1) * D:(which * 2 + 2) * D, :JT] for j in range(J)]
        spread = jnp.concatenate(
            [jnp.broadcast_to(w[j][t:t + 1], (C, JT)) for t in range(D) for j in range(J)], axis=0)
        return hot(b, which) * spread

    def halves(full):
        high = full.astype(BF)
        return high, (full - high.astype(F32)).astype(BF)

    def rows_at(ref, index):
        return ref.at[pl.ds(pl.multiple_of(index * JC, 16), JC)]

    def place(e, b):
        return b * D + e

    def disp_copy(s, b, k):
        t = lax.rem(me + k, D)
        return remote(rows_at(send.at[s], b * D + t), rows_at(recvs[s], place(own, b)),
                      disp_s.at[s, b * D + t], disp_r.at[s, place(own, b)], target(t))

    def disp_in(s, b, k):
        at = place(lax.rem(own + k, D), b)
        return remote(rows_at(send.at[s], 0), rows_at(recvs[s], at),
                      disp_s.at[s, 0], disp_r.at[s, at], target(lax.rem(me + k, D)))

    def own_copy(s, b):
        return pltpu.make_async_copy(
            rows_at(send.at[s], b * D + me), rows_at(recvs[s], place(own, b)), own_sem.at[s, b])

    def span(index, size):
        return pl.ds(pl.multiple_of(index * size, size), size)

    tp = tile_of(width, 512)

    def pack(s, h, zp):
        b, q = zp * H + h, h * ZP + zp
        at = span(b, DC)
        pick = hot(q, 0 if s == 2 else 1).astype(BF)
        factor = jnp.sum(weighted(q, 1), axis=1, keepdims=True) if s == 1 else None

        def one(c):
            cols = span(c, tp)
            total = mm(pick, gath[s, pl.ds(q * J, J), :, cols].reshape(JT, tp))
            if s == 1:
                total = total * factor
            send[s, at, cols] = total.astype(BF)

        loop(width // tp, one)
        loop(D - 1, lambda k: disp_copy(s, b, k + 1).start())
        own_copy(s, b).start()

    def landed(s, r):
        for side in range(2):
            @pl.when((zo - r >= 0) if side else (zo + r < Z))
            def _():
                z = zo - r if side else zo + r
                line_copy(s, side, r).wait_recv()
                for h in range(1, H):
                    dense_copy(s, h, z).start()
                if s == 0:
                    tab_copy(0, lax.rem(zo + Z - z, Z)).wait()

    def onward(s, r):
        along(s, r, lambda copy: copy.start())

    def direct(s, m):
        pack(s, 0, lax.rem(zq + ZP - m, ZP))

    def relay(s, m):
        zp = lax.rem(zq + ZP - m, ZP)
        for h in range(1, H):
            for j in range(J):
                z = zp * J + j
                if s == 0:
                    tab_copy(across(h), lax.rem(zo + Z - z, Z)).wait()
                dense_copy(s, across(h), z).wait_recv()
            pack(s, h, zp)

    def arrive(s, m):
        zp = lax.rem(zq + ZP - m, ZP)

        def one(h):
            b = zp * H + h
            loop(D - 1, lambda k: disp_in(s, b, k + 1).wait_recv())
            loop(D - 1, lambda k: disp_copy(s, b, k + 1).wait_send())
            own_copy(s, b).wait()

        loop(H, one)
        if s > 0:
            loop(D - 1, lambda k: pl.semaphore_signal(
                free.at[s - 1, m], inc=1, device_id=target(lax.rem(me + k + 1, D)), device_id_type=MESH))

    tf = tile_of(ff, 256)
    tw = tile_of(width, 256)
    chunk = H * D * JC
    results = (rf, send.at[0])
    backs = (send.at[2], send.at[1])

    def ret_copy(s, b, k):
        e = lax.rem(own + k, D)
        l = e // H
        p, d, step_p, step_d = axes_of(l)
        at = b * D + p * L + low
        return remote(rows_at(results[s], place(e, b)), rows_at(backs[s], at),
                      ret_s.at[s, place(e, b)], ret_r.at[s, at],
                      (lax.rem(e, H) * step_p + d * step_d, zo * L + l))

    def ret_in(s, b, k):
        t = lax.rem(me + k, D)
        return remote(rows_at(results[s], 0), rows_at(backs[s], b * D + t),
                      ret_s.at[s, 0], ret_r.at[s, b * D + t], target(t))

    def own_back(s, b):
        return pltpu.make_async_copy(
            rows_at(results[s], place(own, b)), rows_at(backs[s], b * D + me), own_sem.at[3 + s, b])

    def give_back(s, m):
        zp = lax.rem(zq + ZP - m, ZP)
        pl.semaphore_wait(free.at[1 - s, m], D - 1)

        def one(n):
            b = zp * H + lax.rem(n + 1, H)
            loop(D - 1, lambda k: ret_copy(s, b, k + 1).start())
            own_back(s, b).start()

        loop(H, one)

    def bwd_rows(m):
        at = span(lax.rem(zq + ZP - m, ZP), chunk)

        def hidden_tile(j):
            cols = span(j, tf)
            ups = pl.ds(pl.multiple_of(ff + j * tf, 128), tf)
            gate = mm(rb_ref[at], win_ref[:, cols])
            up = mm(rb_ref[at], win_ref[:, ups])
            d_hid = mm_cols(rc_ref[at], wdn_ref[cols])
            sig = jax.nn.sigmoid(gate)
            hid_ref[at, cols] = (gate * sig * up).astype(BF)
            dpr_ref[at, cols] = (d_hid * up * sig * (1.0 + gate * (1.0 - sig))).astype(BF)
            dpr_ref[at, ups] = (d_hid * gate * sig).astype(BF)

        loop(ff // tf, hidden_tile)

        def grad_tile(j):
            cols = span(j, tw)
            results[1][at, cols] = mm_cols(dpr_ref[at], win_ref[cols]).astype(BF)

        loop(width // tw, grad_tile)


    def fwd_rows(m):
        at = span(lax.rem(zq + ZP - m, ZP), chunk)

        def hidden_tile(j):
            cols = span(j, tf)
            gate = mm(rf[at], win_ref[:, cols])
            up = mm(rf[at], win_ref[:, pl.ds(pl.multiple_of(ff + j * tf, 128), tf)])
            stage[pl.ds(0, chunk), cols] = (gate * jax.nn.sigmoid(gate) * up).astype(BF)

        loop(ff // tf, hidden_tile)

        def out_tile(j):
            cols = span(j, tw)
            rf[at, cols] = mm(stage[pl.ds(0, chunk), pl.ds(0, ff)], wdn_ref[:, cols]).astype(BF)

        loop(width // tw, out_tile)

    def near_copy(s, h, zp):
        return remote(gath.at[s, pl.ds((h * ZP + zp) * J, J)],
                      near.at[s, pl.ds(((across(h) - 1) * ZP + zp) * J, J)],
                      near_s.at[s, h, zp], near_r.at[s, h, zp], holder(h, zo))

    def gathered(s, h, zp, sides=()):
        b, q = zp * H + h, h * ZP + zp
        loop(D - 1, lambda k: ret_in(s, b, k + 1).wait_recv())
        own_back(s, b).wait()
        for wait, _ in sides:
            wait()
        at = span(b, DC)
        picks = halves(weighted(q, 0)) if s == 0 else (hot(q, 1).astype(BF),)

        def one(c):
            cols = span(c, tp)
            value = backs[s][at, cols]
            total = mm_rows(picks[0], value)
            for more in picks[1:]:
                total = total + mm_rows(more, value)
            for _, first in sides:
                total = total + near[s, pl.ds(first, J), :, cols].reshape(JT, tp).astype(F32)
            gath[s, pl.ds(q * J, J), :, cols] = total.astype(BF).reshape(J, T, tp)

        loop(width // tp, one)

    def half_way(s, m):
        zp = lax.rem(zq + ZP - m, ZP)
        for h in range(1, H):
            gathered(s, h, zp)
            near_copy(s, h, zp).start()

    def part_copy(s, k):
        z = lax.rem(zo + k, Z)
        return remote(gath.at[s, z], parts.at[s, zo], part_s.at[s, k], part_r.at[s, k], holder(0, z))

    def settle(s):
        for h in range(1, H):
            loop(Z, lambda z: dense_copy(s, h, z).wait_send())
        for r in range(Z - 1):
            along(s, r, lambda copy: copy.wait_send())

    def combine(s, m):
        zp = lax.rem(zq + ZP - m, ZP)
        gathered(s, 0, zp, [(near_copy(s, across(h), zp).wait_recv, ((h - 1) * ZP + zp) * J)
                            for h in range(1, H)])
        for j in range(0 if m else 1, J):
            part_copy(s, lax.rem(zp * J + lax.rem(zj + j, J) + Z - zo, Z)).start()
        if m == 0:
            parts[s, zo] = gath[s, zo]

    tg = math.gcd(tf, tw)
    count_in, count_down = width // tg, ff // tg

    def in_copy(j):
        slot = lax.rem(j, 2)
        return pltpu.make_async_copy(
            stage.at[span(slot, tg), pl.ds(0, 2 * ff)], gin_hbm.at[span(j, tg)], stage_sem.at[slot])

    def down_copy(j):
        slot = lax.rem(j, 2)
        return pltpu.make_async_copy(
            stage.at[span(slot, tg), pl.ds(0, width)], gdn_hbm.at[span(j, tg)], stage_sem.at[slot])

    def in_tile(j):
        value = mm_rows(rb_ref[:, span(j, tg)], dpr_ref[...]).astype(BF)

        @pl.when(j >= 2)
        def _():
            in_copy(j - 2).wait()

        stage[span(lax.rem(j, 2), tg), pl.ds(0, 2 * ff)] = value
        in_copy(j).start()

    def finish_in():
        for j in range(max(0, count_in - 2), count_in):
            in_copy(j).wait()

    def down_tile(j):
        value = mm_rows(hid_ref[:, span(j, tg)], rc_ref[...]).astype(BF)

        @pl.when(j >= 2)
        def _():
            down_copy(j - 2).wait()

        stage[span(lax.rem(j, 2), tg), pl.ds(0, width)] = value
        down_copy(j).start()

    far = range(1, ZP)
    for s in range(3):
        landed(s, 1)
        if s < 2:
            onward(s + 1, 0)
        else:
            onward(0, 1)
        direct(s, 0)
        if s > 0:
            relay(s - 1, 0)
    relay(2, 0)
    for s in range(3):
        landed(s, 2)
        onward(s, 2)
        if s < 2:
            onward(s + 1, 1)
        for r in range(3, Z):
            landed(s, r)
            onward(s, r)
        for m in far:
            direct(s, m)
        if s > 0:
            for m in far:
                relay(s - 1, m)
        if s == 1:
            arrive(0, 0)
            arrive(1, 0)
            load_in.wait()
            load_down.wait()
            bwd_rows(0)
    for m in far:
        relay(2, m)
    arrive(2, 0)
    give_back(1, 0)
    for m in far:
        arrive(0, m)
        arrive(1, m)
        bwd_rows(m)
        give_back(1, m)
    for m in far:
        arrive(2, m)
        fwd_rows(m)
        give_back(0, m)
    settle(1)
    settle(0)
    fwd_rows(0)
    for m in far:
        half_way(1, m)
    for m in far:
        half_way(0, m)
    for m in far:
        combine(1, m)
    give_back(0, 0)
    half_way(1, 0)
    for m in far:
        combine(0, m)
    loop(count_in, in_tile)
    finish_in()
    half_way(0, 0)
    combine(1, 0)
    loop(count_down, down_tile)
    for j in range(max(0, count_down - 2), count_down):
        down_copy(j).wait()
    combine(0, 0)
    for s, out in ((1, gt_ref), (0, of_ref)):
        loop(Z - 1, lambda k: part_copy(s, k + 1).wait())
        total = parts[s, 0].astype(F32)
        for z in range(1, Z):
            total = total + parts[s, z].astype(F32)
        out[...] = total.astype(BF)
    for r in range(Z - 1):
        along(2, r, lambda copy: copy.wait_send())
    for s in range(2):
        def sent(b, s=s):
            loop(D - 1, lambda k: ret_copy(s, b, k + 1).wait_send())

        loop(B, sent)
        for h in range(1, H):
            loop(ZP, lambda zp: near_copy(s, h, zp).wait_send())
    for h in range(1, H):
        loop(Z, lambda z: dense_copy(2, h, z).wait_send())


def hand_over(*refs):
    sources, targets, (held_in, held_down, held_tok, in_sem, out_sem) = refs[:4], refs[4:8], refs[8:]
    helds = (held_tok.at[0], held_tok.at[1], held_in, held_down)
    moves = []
    for n, (src, held, dst) in enumerate(zip(sources, helds, targets)):
        pieces = PIECES if src.shape[0] % (16 * PIECES) == 0 else 1
        size = src.shape[0] // pieces
        for p in range(pieces):
            at = pl.ds(p * size, size)
            moves.append((pltpu.make_async_copy(src.at[at], held.at[at], in_sem.at[n, p]),
                          pltpu.make_async_copy(held.at[at], dst.at[at], out_sem.at[n, p])))
    for load, _ in moves:
        load.start()
    for load, store in moves:
        load.wait()
        store.start()
    for _, store in moves:
        store.wait()


def shards(tokens_fwd, experts_fwd, scores_fwd, tokens_bwd, experts_bwd, scores_bwd,
           cotangent, w_in, w_down):
    G, inner = lax.axis_size("group"), lax.axis_size("inner")
    n = G * inner
    T, top = experts_fwd.shape
    width = tokens_fwd.shape[1]
    ff = w_down.shape[1]
    capacity = max(2, 3 * T * top // (2 * n))
    C = -(-capacity // 8) * 8
    Z = max(d for d in range(1, inner + 1) if inner % d == 0 and d * d <= n)
    L = inner // Z
    H = math.isqrt(G)
    assert H * H == G
    D = H * L
    rows = n * C
    J = 2
    assert Z % J == 0
    lanes = -(-J * T // 128) * 128
    vmem = pl.BlockSpec(memory_space=pltpu.VMEM)
    dma = pltpu.SemaphoreType.DMA
    hbm = pl.BlockSpec(memory_space=pl.ANY)
    tg = math.gcd(tile_of(ff, 256), tile_of(width, 256))
    results = pl.pallas_call(
        functools.partial(layer_kernel, (Z, H, L, C, T, J, inner)),
        out_shape=(
            jax.ShapeDtypeStruct((T, width), BF),
            jax.ShapeDtypeStruct((T, width), BF),
            jax.ShapeDtypeStruct((width, 2 * ff), BF),
            jax.ShapeDtypeStruct((ff, width), BF),
        ),
        in_specs=[vmem] * 7 + [hbm] * 2,
        out_specs=(vmem, vmem, hbm, hbm),
        scratch_shapes=[
            pltpu.VMEM((H * Z, 4 * D, lanes), F32),
            pltpu.VMEM((H * Z, 4 * D, lanes), F32),
            pltpu.VMEM((width, 2 * ff), BF),
            pltpu.VMEM((ff, width), BF),
            pltpu.VMEM((rows, width), BF),
            pltpu.VMEM((rows, width), BF),
            pltpu.VMEM((rows, width), BF),
            pltpu.VMEM((rows, ff), BF),
            pltpu.VMEM((rows, 2 * ff), BF),
            pltpu.VMEM((3, H * Z, T, width), BF),
            pltpu.VMEM((3, rows, width), BF),
            pltpu.VMEM((2, Z, T, width), BF),
            pltpu.VMEM((2, (H - 1) * Z, T, width), BF),
            pltpu.VMEM((max(2 * tg, rows // 2), max(2 * ff, width)), BF),
            dma((2,)),
            dma((5, H * Z)), dma((2,)), dma((H, Z)), dma((H, Z)), dma((3, 2, Z)), dma((3, Z)),
            dma((3, H, Z)), dma((3, H, Z)), dma((3, n)), dma((3, n)),
            dma((2, n)), dma((2, n)), dma((2, H, Z)), dma((2, H, Z)), dma((2, Z)), dma((2, Z)),
            pltpu.SemaphoreType.REGULAR((2, Z // J)),
        ],
        compiler_params=pltpu.CompilerParams(
            collective_id=0, has_side_effects=True, vmem_limit_bytes=67043328),
        name="moe_layer",
    )(experts_fwd.T, scores_fwd.T, experts_bwd.T, scores_bwd.T, tokens_bwd, cotangent, tokens_fwd, w_in[0], w_down[0])
    out_fwd, grad_tok, grad_in, grad_down = pl.pallas_call(
        hand_over,
        out_shape=tuple(jax.ShapeDtypeStruct(r.shape, r.dtype) for r in results),
        in_specs=[hbm] * 4,
        out_specs=(hbm,) * 4,
        scratch_shapes=[
            pltpu.VMEM((width, 2 * ff), BF), pltpu.VMEM((ff, width), BF), pltpu.VMEM((2, T, width), BF),
            dma((4, PIECES)), dma((4, PIECES)),
        ],
        compiler_params=pltpu.CompilerParams(vmem_limit_bytes=2 ** 24),
        name="hand_over",
    )(*results)
    return out_fwd, grad_tok, grad_in[None], grad_down[None]


def solution(mesh):
    two, three = P(("group", "inner"), None), P(("group", "inner"), None, None)
    return jax.shard_map(
        shards, mesh=mesh,
        in_specs=(two,) * 7 + (three,) * 2,
        out_specs=(two, two, three, three),
        check_vma=False,
    )
```

```python
import functools
import math

import jax
import jax.numpy as jnp
from jax import lax
from jax.experimental import pallas as pl
from jax.experimental.pallas import tpu as pltpu
from jax.sharding import PartitionSpec as P

MESH = pl.DeviceIdType.MESH
BF = jnp.bfloat16
F32 = jnp.float32
PIECES = 8
ROWS = (((0,), (0,)), ((), ()))
COLS = (((1,), (1,)), ((), ()))


def mm(a, b):
    return jnp.dot(a, b, preferred_element_type=F32)


def mm_rows(a, b):
    return lax.dot_general(a, b, ROWS, preferred_element_type=F32)


def mm_cols(a, b):
    return lax.dot_general(a, b, COLS, preferred_element_type=F32)


def tile_of(size, most):
    return max(t for t in range(128, most + 1, 128) if size % t == 0)


def loop(count, body):
    lax.fori_loop(0, count, lambda k, c: (body(k), c)[1], 0)


def layer_kernel(dims, idf_hbm, scf_hbm, idb_hbm, scb_hbm, xb_hbm, ct_hbm, xf_hbm, win_hbm, wdn_hbm,
                 of_hbm, gt_hbm, gin_hbm, gdn_hbm, id_ref, sc_ref, out_ref, load_sem,
                 tab_ref, tabs, win_ref, wdn_ref, rb_ref, rc_ref, rf, hid_ref, dpr_ref,
                 gath, send, parts, near, stage, stage_sem, own_sem, w_sem,
                 tab_s, tab_r, gath_s, gath_r, dense_s, dense_r, disp_s, disp_r,
                 ret_s, ret_r, near_s, near_r, part_s, part_r, free):
    Z, H, L, C, T, J, inner = dims
    D = H * L
    ZP, JC, JT = Z // J, J * C, J * T
    B = H * ZP
    DC = D * JC
    ff, width = wdn_ref.shape
    load_in = pltpu.make_async_copy(win_hbm, win_ref, w_sem.at[0])
    load_down = pltpu.make_async_copy(wdn_hbm, wdn_ref, w_sem.at[1])
    g = lax.axis_index("group")
    i = lax.axis_index("inner")
    zo, low = i // L, lax.rem(i, L)
    zq, zj = zo // J, lax.rem(zo, J)
    first, second = g // H, lax.rem(g, H)

    def axes_of(l):
        odd = lax.rem(l, 2)
        pack = first * (1 - odd) + second * odd
        dense = second * (1 - odd) + first * odd
        return pack, dense, H - odd * (H - 1), 1 + odd * (H - 1)

    pc, dc, sp, sd = axes_of(low)
    me = pc * L + low
    own = low * H + pc
    A = H * D
    ma = g * L + low

    def plane(a):
        return (a // L, zo * L + lax.rem(a, L))

    def holder(h, z):
        return (pc * sp + lax.rem(dc + h, H) * sd, z * L + low)

    def target(t):
        return ((t // L) * sp + dc * sd, zo * L + lax.rem(t, L))

    loads = [pltpu.make_async_copy(src, dst, load_sem.at[n]) for n, (src, dst) in enumerate((
        (xb_hbm, gath.at[0, zo]), (ct_hbm, gath.at[1, zo]), (xf_hbm, gath.at[2, zo]),
        (idf_hbm, id_ref.at[0]), (scf_hbm, sc_ref.at[0]),
        (idb_hbm, id_ref.at[1]), (scb_hbm, sc_ref.at[1])))]
    for load in loads:
        load.start()
    barrier = pltpu.get_barrier_semaphore()

    def greet(device):
        pl.semaphore_signal(barrier, inc=1, device_id=device, device_id_type=MESH)

    loop(A - 1, lambda k: greet(plane(lax.rem(ma + k + 1, A))))
    for h in range(H):
        loop(Z - 1, lambda k: greet(holder(h, lax.rem(zo + k + 1, Z))))

    def remote(src, dst, ssem, rsem, device):
        return pltpu.make_async_remote_copy(
            src_ref=src, dst_ref=dst, send_sem=ssem, recv_sem=rsem,
            device_id=device, device_id_type=MESH)

    recvs = (rb_ref, rc_ref, rf)

    def across(h):
        return (H - h) % H

    def tab_copy(h, k):
        z = lax.rem(zo + k, Z)
        return remote(tab_ref.at[h * Z + z], tabs.at[across(h) * Z + zo],
                      tab_s.at[h, k], tab_r.at[h, k], holder(h, z))

    def line_copy(s, side, r):
        z = zo - r if side else zo + r
        return remote(gath.at[s, z], gath.at[s, z], gath_s.at[s, side, r], gath_r.at[s, z],
                      holder(0, zo + 1 if side else zo - 1))

    def along(s, r, act):
        @pl.when((zo + 1 < Z) & (zo - r >= 0))
        def _():
            act(line_copy(s, 1, r))

        @pl.when((zo >= 1) & (zo + r < Z))
        def _():
            act(line_copy(s, 0, r))

    def dense_copy(s, h, z):
        return remote(gath.at[s, z], gath.at[s, across(h) * Z + z],
                      dense_s.at[s, h, z], dense_r.at[s, h, z], holder(h, zo))

    for load in loads:
        load.wait()
    pl.semaphore_wait(barrier, A - 1 + H * (Z - 1))
    for s in range(3):
        for h in range(1, H):
            dense_copy(s, h, zo).start()
    along(0, 0, lambda copy: copy.start())
    load_in.start()
    load_down.start()

    row = lax.broadcasted_iota(jnp.int32, (H * Z * D, JT), 0)
    h_of, z_of, t_of = row // (Z * D), (row // D) % Z, row % D
    g_of = (t_of // L) * sp + ((dc + h_of) % H) * sd
    expert = (g_of * inner + z_of * L + t_of % L).astype(F32)
    mine = lax.broadcasted_iota(jnp.int32, (1, JT), 1) // T == zj
    earlier = (lax.broadcasted_iota(jnp.int32, (JT, JT), 0)
               < lax.broadcasted_iota(jnp.int32, (JT, JT), 1)).astype(F32).astype(BF)
    tab_ref[...] = jnp.zeros_like(tab_ref)
    for which in range(2):
        ids = jnp.where(mine, jnp.concatenate([id_ref[which].astype(F32)] * J, axis=1), -1.0)
        scores = jnp.concatenate([sc_ref[which]] * J, axis=1)
        weights = scores / jnp.sum(scores, axis=0, keepdims=True)
        named = jnp.zeros((H * Z * D, JT), F32)
        weight = jnp.zeros((H * Z * D, JT), F32)
        for k in range(ids.shape[0]):
            hit = jnp.broadcast_to(ids[k:k + 1], (H * Z * D, JT)) == expert
            named = named + hit.astype(F32)
            weight = weight + jnp.where(hit, jnp.broadcast_to(weights[k:k + 1], (H * Z * D, JT)), 0.0)
        slot = jnp.where(named > 0.5, mm(named.astype(BF), earlier), -1.0)
        for b in range(H * Z):
            tab_ref[b, 2 * which * D:(2 * which + 1) * D, :JT] = slot[b * D:(b + 1) * D]
            tab_ref[b, (2 * which + 1) * D:(2 * which + 2) * D, :JT] = weight[b * D:(b + 1) * D]

    loop(Z - 1, lambda k: tab_copy(0, k + 1).start())
    for h in range(1, H):
        loop(Z, lambda k: tab_copy(h, k).start())
    tabs[zo] = tab_ref[zo]

    def hot(b, which):
        slots = [tabs[b * J + j, which * 2 * D:(which * 2 + 1) * D, :JT] for j in range(J)]
        want = lax.broadcasted_iota(jnp.int32, (C, JT), 0).astype(F32)
        return jnp.concatenate(
            [(jnp.broadcast_to(slots[j][t:t + 1], (C, JT)) == want).astype(F32)
             for t in range(D) for j in range(J)], axis=0)

    def weighted(b, which):
        w = [tabs[b * J + j, (which * 2 + 1) * D:(which * 2 + 2) * D, :JT] for j in range(J)]
        spread = jnp.concatenate(
            [jnp.broadcast_to(w[j][t:t + 1], (C, JT)) for t in range(D) for j in range(J)], axis=0)
        return hot(b, which) * spread

    def halves(full):
        high = full.astype(BF)
        return high, (full - high.astype(F32)).astype(BF)

    def rows_at(ref, index):
        return ref.at[pl.ds(pl.multiple_of(index * JC, 16), JC)]

    def place(e, b):
        return b * D + e

    def disp_copy(s, b, k):
        t = lax.rem(me + k, D)
        return remote(rows_at(send.at[s], b * D + t), rows_at(recvs[s], place(own, b)),
                      disp_s.at[s, b * D + t], disp_r.at[s, place(own, b)], target(t))

    def disp_in(s, b, k):
        at = place(lax.rem(own + k, D), b)
        return remote(rows_at(send.at[s], 0), rows_at(recvs[s], at),
                      disp_s.at[s, 0], disp_r.at[s, at], target(lax.rem(me + k, D)))

    def own_copy(s, b):
        return pltpu.make_async_copy(
            rows_at(send.at[s], b * D + me), rows_at(recvs[s], place(own, b)), own_sem.at[s, b])

    def span(index, size):
        return pl.ds(pl.multiple_of(index * size, size), size)

    tp = tile_of(width, 512)

    def pack(s, h, zp):
        b, q = zp * H + h, h * ZP + zp
        at = span(b, DC)
        pick = hot(q, 0 if s == 2 else 1).astype(BF)
        factor = jnp.sum(weighted(q, 1), axis=1, keepdims=True) if s == 1 else None

        def one(c):
            cols = span(c, tp)
            total = mm(pick, gath[s, pl.ds(q * J, J), :, cols].reshape(JT, tp))
            if s == 1:
                total = total * factor
            send[s, at, cols] = total.astype(BF)

        loop(width // tp, one)
        loop(D - 1, lambda k: disp_copy(s, b, k + 1).start())
        own_copy(s, b).start()

    def landed(s, r):
        for side in range(2):
            @pl.when((zo - r >= 0) if side else (zo + r < Z))
            def _():
                z = zo - r if side else zo + r
                line_copy(s, side, r).wait_recv()
                for h in range(1, H):
                    dense_copy(s, h, z).start()
                if s == 0:
                    tab_copy(0, lax.rem(zo + Z - z, Z)).wait()

    def onward(s, r):
        along(s, r, lambda copy: copy.start())

    def direct(s, m):
        pack(s, 0, lax.rem(zq + ZP - m, ZP))

    def relay(s, m):
        zp = lax.rem(zq + ZP - m, ZP)
        for h in range(1, H):
            for j in range(J):
                z = zp * J + j
                if s == 0:
                    tab_copy(across(h), lax.rem(zo + Z - z, Z)).wait()
                dense_copy(s, across(h), z).wait_recv()
            pack(s, h, zp)

    def arrive(s, m):
        zp = lax.rem(zq + ZP - m, ZP)

        def one(h):
            b = zp * H + h
            loop(D - 1, lambda k: disp_in(s, b, k + 1).wait_recv())
            loop(D - 1, lambda k: disp_copy(s, b, k + 1).wait_send())
            own_copy(s, b).wait()

        loop(H, one)
        if s > 0:
            loop(D - 1, lambda k: pl.semaphore_signal(
                free.at[s - 1, m], inc=1, device_id=target(lax.rem(me + k + 1, D)), device_id_type=MESH))

    tf = tile_of(ff, 256)
    tw = tile_of(width, 256)
    chunk = H * D * JC
    results = (rf, send.at[0])
    backs = (send.at[2], send.at[1])

    def ret_copy(s, b, k):
        e = lax.rem(own + k, D)
        l = e // H
        p, d, step_p, step_d = axes_of(l)
        at = b * D + p * L + low
        return remote(rows_at(results[s], place(e, b)), rows_at(backs[s], at),
                      ret_s.at[s, place(e, b)], ret_r.at[s, at],
                      (lax.rem(e, H) * step_p + d * step_d, zo * L + l))

    def ret_in(s, b, k):
        t = lax.rem(me + k, D)
        return remote(rows_at(results[s], 0), rows_at(backs[s], b * D + t),
                      ret_s.at[s, 0], ret_r.at[s, b * D + t], target(t))

    def own_back(s, b):
        return pltpu.make_async_copy(
            rows_at(results[s], place(own, b)), rows_at(backs[s], b * D + me), own_sem.at[3 + s, b])

    def give_back(s, m):
        zp = lax.rem(zq + ZP - m, ZP)
        pl.semaphore_wait(free.at[1 - s, m], D - 1)

        def one(n):
            b = zp * H + lax.rem(n + 1, H)
            loop(D - 1, lambda k: ret_copy(s, b, k + 1).start())
            own_back(s, b).start()

        loop(H, one)

    def bwd_rows(m):
        at = span(lax.rem(zq + ZP - m, ZP), chunk)

        def hidden_tile(j):
            cols = span(j, tf)
            ups = pl.ds(pl.multiple_of(ff + j * tf, 128), tf)
            gate = mm(rb_ref[at], win_ref[:, cols])
            up = mm(rb_ref[at], win_ref[:, ups])
            d_hid = mm_cols(rc_ref[at], wdn_ref[cols])
            sig = jax.nn.sigmoid(gate)
            hid_ref[at, cols] = (gate * sig * up).astype(BF)
            dpr_ref[at, cols] = (d_hid * up * sig * (1.0 + gate * (1.0 - sig))).astype(BF)
            dpr_ref[at, ups] = (d_hid * gate * sig).astype(BF)

        loop(ff // tf, hidden_tile)

        def grad_tile(j):
            cols = span(j, tw)
            results[1][at, cols] = mm_cols(dpr_ref[at], win_ref[cols]).astype(BF)

        loop(width // tw, grad_tile)


    def fwd_rows(m):
        at = span(lax.rem(zq + ZP - m, ZP), chunk)

        def hidden_tile(j):
            cols = span(j, tf)
            gate = mm(rf[at], win_ref[:, cols])
            up = mm(rf[at], win_ref[:, pl.ds(pl.multiple_of(ff + j * tf, 128), tf)])
            stage[pl.ds(0, chunk), cols] = (gate * jax.nn.sigmoid(gate) * up).astype(BF)

        loop(ff // tf, hidden_tile)

        def out_tile(j):
            cols = span(j, tw)
            rf[at, cols] = mm(stage[pl.ds(0, chunk), pl.ds(0, ff)], wdn_ref[:, cols]).astype(BF)

        loop(width // tw, out_tile)

    def near_copy(s, h, zp):
        return remote(gath.at[s, pl.ds((h * ZP + zp) * J, J)],
                      near.at[s, pl.ds(((across(h) - 1) * ZP + zp) * J, J)],
                      near_s.at[s, h, zp], near_r.at[s, h, zp], holder(h, zo))

    def gathered(s, h, zp, sides=()):
        b, q = zp * H + h, h * ZP + zp
        loop(D - 1, lambda k: ret_in(s, b, k + 1).wait_recv())
        own_back(s, b).wait()
        for wait, _ in sides:
            wait()
        at = span(b, DC)
        picks = halves(weighted(q, 0)) if s == 0 else (hot(q, 1).astype(BF),)

        def one(c):
            cols = span(c, tp)
            value = backs[s][at, cols]
            total = mm_rows(picks[0], value)
            for more in picks[1:]:
                total = total + mm_rows(more, value)
            for _, first in sides:
                total = total + near[s, pl.ds(first, J), :, cols].reshape(JT, tp).astype(F32)
            gath[s, pl.ds(q * J, J), :, cols] = total.astype(BF).reshape(J, T, tp)

        loop(width // tp, one)

    def half_way(s, m):
        zp = lax.rem(zq + ZP - m, ZP)
        for h in range(1, H):
            gathered(s, h, zp)
            near_copy(s, h, zp).start()

    def part_copy(s, k):
        z = lax.rem(zo + k, Z)
        return remote(gath.at[s, z], parts.at[s, zo], part_s.at[s, k], part_r.at[s, k], holder(0, z))

    def settle(s):
        for h in range(1, H):
            loop(Z, lambda z: dense_copy(s, h, z).wait_send())
        for r in range(Z - 1):
            along(s, r, lambda copy: copy.wait_send())

    def combine(s, m):
        zp = lax.rem(zq + ZP - m, ZP)
        gathered(s, 0, zp, [(near_copy(s, across(h), zp).wait_recv, ((h - 1) * ZP + zp) * J)
                            for h in range(1, H)])
        for j in range(0 if m else 1, J):
            part_copy(s, lax.rem(zp * J + lax.rem(zj + j, J) + Z - zo, Z)).start()
        if m == 0:
            parts[s, zo] = gath[s, zo]

    tg = math.gcd(tf, tw)
    count_in, count_down = width // tg, ff // tg

    def in_copy(j):
        slot = lax.rem(j, 2)
        return pltpu.make_async_copy(
            stage.at[span(slot, tg), pl.ds(0, 2 * ff)], gin_hbm.at[span(j, tg)], stage_sem.at[slot])

    def down_copy(j):
        slot = lax.rem(j, 2)
        return pltpu.make_async_copy(
            stage.at[span(slot, tg), pl.ds(0, width)], gdn_hbm.at[span(j, tg)], stage_sem.at[slot])

    def in_tile(j):
        value = mm_rows(rb_ref[:, span(j, tg)], dpr_ref[...]).astype(BF)

        @pl.when(j >= 2)
        def _():
            in_copy(j - 2).wait()

        stage[span(lax.rem(j, 2), tg), pl.ds(0, 2 * ff)] = value
        in_copy(j).start()

    def finish_in():
        for j in range(max(0, count_in - 2), count_in):
            in_copy(j).wait()

    def down_tile(j):
        value = mm_rows(hid_ref[:, span(j, tg)], rc_ref[...]).astype(BF)

        @pl.when(j >= 2)
        def _():
            down_copy(j - 2).wait()

        stage[span(lax.rem(j, 2), tg), pl.ds(0, width)] = value
        down_copy(j).start()

    far = range(1, ZP)
    for s in range(3):
        landed(s, 1)
        if s < 2:
            onward(s + 1, 0)
        else:
            onward(0, 1)
        direct(s, 0)
        if s > 0:
            relay(s - 1, 0)
    relay(2, 0)
    for s in range(3):
        landed(s, 2)
        onward(s, 2)
        if s < 2:
            onward(s + 1, 1)
        for r in range(3, Z):
            landed(s, r)
            onward(s, r)
        for m in far:
            direct(s, m)
        if s > 0:
            for m in far:
                relay(s - 1, m)
        if s == 1:
            arrive(0, 0)
            arrive(1, 0)
            load_in.wait()
            load_down.wait()
            bwd_rows(0)
    for m in far:
        relay(2, m)
    arrive(2, 0)
    give_back(1, 0)
    for m in far:
        arrive(0, m)
        arrive(1, m)
        bwd_rows(m)
        give_back(1, m)
    for m in far:
        arrive(2, m)
        fwd_rows(m)
        give_back(0, m)
    settle(1)
    settle(0)
    fwd_rows(0)
    for m in far:
        half_way(1, m)
    for m in far:
        half_way(0, m)
    for m in far:
        combine(1, m)
    give_back(0, 0)
    half_way(1, 0)
    for m in far:
        combine(0, m)
    loop(count_in, in_tile)
    finish_in()
    half_way(0, 0)
    combine(1, 0)
    loop(count_down, down_tile)
    for j in range(max(0, count_down - 2), count_down):
        down_copy(j).wait()
    combine(0, 0)
    outs = [pltpu.make_async_copy(out_ref.at[s], out, load_sem.at[s]) for s, out in enumerate((of_hbm, gt_hbm))]
    for s in (1, 0):
        loop(Z - 1, lambda k: part_copy(s, k + 1).wait())
        total = parts[s, 0].astype(F32)
        for z in range(1, Z):
            total = total + parts[s, z].astype(F32)
        out_ref[s] = total.astype(BF)
        outs[s].start()
    for r in range(Z - 1):
        along(2, r, lambda copy: copy.wait_send())
    for s in range(2):
        def sent(b, s=s):
            loop(D - 1, lambda k: ret_copy(s, b, k + 1).wait_send())

        loop(B, sent)
        for h in range(1, H):
            loop(ZP, lambda zp: near_copy(s, h, zp).wait_send())
    for h in range(1, H):
        loop(Z, lambda z: dense_copy(2, h, z).wait_send())
    for out in outs:
        out.wait()


def hand_over(*refs):
    sources, targets, (held_in, held_down, held_tok, in_sem, out_sem) = refs[:4], refs[4:8], refs[8:]
    helds = (held_tok.at[0], held_tok.at[1], held_in, held_down)
    moves = []
    for n, (src, held, dst) in enumerate(zip(sources, helds, targets)):
        pieces = PIECES if src.shape[0] % (16 * PIECES) == 0 else 1
        size = src.shape[0] // pieces
        for p in range(pieces):
            at = pl.ds(p * size, size)
            moves.append((pltpu.make_async_copy(src.at[at], held.at[at], in_sem.at[n, p]),
                          pltpu.make_async_copy(held.at[at], dst.at[at], out_sem.at[n, p])))
    for load, _ in moves:
        load.start()
    for load, store in moves:
        load.wait()
        store.start()
    for _, store in moves:
        store.wait()


def shards(tokens_fwd, experts_fwd, scores_fwd, tokens_bwd, experts_bwd, scores_bwd,
           cotangent, w_in, w_down):
    G, inner = lax.axis_size("group"), lax.axis_size("inner")
    n = G * inner
    T, top = experts_fwd.shape
    width = tokens_fwd.shape[1]
    ff = w_down.shape[1]
    capacity = max(2, 3 * T * top // (2 * n))
    C = -(-capacity // 8) * 8
    Z = max(d for d in range(1, inner + 1) if inner % d == 0 and d * d <= n)
    L = inner // Z
    H = math.isqrt(G)
    assert H * H == G
    D = H * L
    rows = n * C
    J = 2
    assert Z % J == 0
    lanes = -(-J * T // 128) * 128
    dma = pltpu.SemaphoreType.DMA
    hbm = pl.BlockSpec(memory_space=pl.ANY)
    tg = math.gcd(tile_of(ff, 256), tile_of(width, 256))
    results = pl.pallas_call(
        functools.partial(layer_kernel, (Z, H, L, C, T, J, inner)),
        out_shape=(
            jax.ShapeDtypeStruct((T, width), BF),
            jax.ShapeDtypeStruct((T, width), BF),
            jax.ShapeDtypeStruct((width, 2 * ff), BF),
            jax.ShapeDtypeStruct((ff, width), BF),
        ),
        in_specs=[hbm] * 9,
        out_specs=(hbm,) * 4,
        scratch_shapes=[
            pltpu.VMEM((2, top, T), jnp.int32), pltpu.VMEM((2, top, T), F32),
            pltpu.VMEM((2, T, width), BF), dma((7,)),
            pltpu.VMEM((H * Z, 4 * D, lanes), F32),
            pltpu.VMEM((H * Z, 4 * D, lanes), F32),
            pltpu.VMEM((width, 2 * ff), BF),
            pltpu.VMEM((ff, width), BF),
            pltpu.VMEM((rows, width), BF),
            pltpu.VMEM((rows, width), BF),
            pltpu.VMEM((rows, width), BF),
            pltpu.VMEM((rows, ff), BF),
            pltpu.VMEM((rows, 2 * ff), BF),
            pltpu.VMEM((3, H * Z, T, width), BF),
            pltpu.VMEM((3, rows, width), BF),
            pltpu.VMEM((2, Z, T, width), BF),
            pltpu.VMEM((2, (H - 1) * Z, T, width), BF),
            pltpu.VMEM((max(2 * tg, rows // 2), max(2 * ff, width)), BF),
            dma((2,)),
            dma((5, H * Z)), dma((2,)), dma((H, Z)), dma((H, Z)), dma((3, 2, Z)), dma((3, Z)),
            dma((3, H, Z)), dma((3, H, Z)), dma((3, n)), dma((3, n)),
            dma((2, n)), dma((2, n)), dma((2, H, Z)), dma((2, H, Z)), dma((2, Z)), dma((2, Z)),
            pltpu.SemaphoreType.REGULAR((2, Z // J)),
        ],
        compiler_params=pltpu.CompilerParams(
            collective_id=0, has_side_effects=True, vmem_limit_bytes=67043328),
        name="moe_layer",
    )(experts_fwd.T, scores_fwd.T, experts_bwd.T, scores_bwd.T, tokens_bwd, cotangent, tokens_fwd, w_in[0], w_down[0])
    out_fwd, grad_tok, grad_in, grad_down = pl.pallas_call(
        hand_over,
        out_shape=tuple(jax.ShapeDtypeStruct(r.shape, r.dtype) for r in results),
        in_specs=[hbm] * 4,
        out_specs=(hbm,) * 4,
        scratch_shapes=[
            pltpu.VMEM((width, 2 * ff), BF), pltpu.VMEM((ff, width), BF), pltpu.VMEM((2, T, width), BF),
            dma((4, PIECES)), dma((4, PIECES)),
        ],
        compiler_params=pltpu.CompilerParams(vmem_limit_bytes=67043328),
        name="hand_over",
    )(*results)
    return out_fwd, grad_tok, grad_in[None], grad_down[None]


def solution(mesh):
    two, three = P(("group", "inner"), None), P(("group", "inner"), None, None)
    return jax.shard_map(
        shards, mesh=mesh,
        in_specs=(two,) * 7 + (three,) * 2,
        out_specs=(two, two, three, three),
        check_vma=False,
    )
```

```python
import functools
import math

import jax
import jax.numpy as jnp
from jax import lax
from jax.experimental import pallas as pl
from jax.experimental.pallas import tpu as pltpu
from jax.sharding import PartitionSpec as P

MESH = pl.DeviceIdType.MESH
BF = jnp.bfloat16
F32 = jnp.float32
PIECES = 8
ROWS = (((0,), (0,)), ((), ()))
COLS = (((1,), (1,)), ((), ()))


def mm(a, b):
    return jnp.dot(a, b, preferred_element_type=F32)


def mm_rows(a, b):
    return lax.dot_general(a, b, ROWS, preferred_element_type=F32)


def mm_cols(a, b):
    return lax.dot_general(a, b, COLS, preferred_element_type=F32)


def tile_of(size, most):
    return max(t for t in range(128, most + 1, 128) if size % t == 0)


def loop(count, body):
    lax.fori_loop(0, count, lambda k, c: (body(k), c)[1], 0)


def layer_kernel(dims, idf_hbm, scf_hbm, idb_hbm, scb_hbm, xb_hbm, ct_hbm, xf_hbm, win_hbm, wdn_hbm,
                 of_hbm, gt_hbm, gin_hbm, gdn_hbm, id_ref, sc_ref, out_ref, load_sem,
                 tab_ref, tabs, win_ref, wdn_ref, rb_ref, rc_ref, rf, hid_ref, dpr_ref,
                 gath, send, parts, near, mate, stage, stage_sem, own_sem, w_sem,
                 tab_s, tab_r, gath_s, gath_r, dense_s, dense_r, disp_s, disp_r,
                 ret_s, ret_r, near_s, near_r, part_s, part_r, pair_s, pair_r, mate_s, mate_r, free):
    Z, H, L, C, T, J, inner = dims
    D = H * L
    ZP, JC, JT = Z // J, J * C, J * T
    B = H * ZP
    DC = D * JC
    ff, width = wdn_ref.shape
    load_in = pltpu.make_async_copy(win_hbm, win_ref, w_sem.at[0])
    load_down = pltpu.make_async_copy(wdn_hbm, wdn_ref, w_sem.at[1])
    g = lax.axis_index("group")
    i = lax.axis_index("inner")
    zo, low = i // L, lax.rem(i, L)
    zq, zj = zo // J, lax.rem(zo, J)
    first, second = g // H, lax.rem(g, H)

    def axes_of(l):
        odd = lax.rem(l, 2)
        pack = first * (1 - odd) + second * odd
        dense = second * (1 - odd) + first * odd
        return pack, dense, H - odd * (H - 1), 1 + odd * (H - 1)

    pc, dc, sp, sd = axes_of(low)
    me = pc * L + low
    own = low * H + pc
    A = H * D
    ma = g * L + low

    def plane(a):
        return (a // L, zo * L + lax.rem(a, L))

    def holder(h, z):
        return (pc * sp + lax.rem(dc + h, H) * sd, z * L + low)

    def target(t):
        return ((t // L) * sp + dc * sd, zo * L + lax.rem(t, L))

    loads = [pltpu.make_async_copy(src, dst, load_sem.at[n]) for n, (src, dst) in enumerate((
        (xb_hbm, gath.at[0, zo]), (ct_hbm, gath.at[1, zo]), (xf_hbm, gath.at[2, zo]),
        (idf_hbm, id_ref.at[0]), (scf_hbm, sc_ref.at[0]),
        (idb_hbm, id_ref.at[1]), (scb_hbm, sc_ref.at[1])))]
    for load in loads:
        load.start()
    barrier = pltpu.get_barrier_semaphore()

    def greet(device):
        pl.semaphore_signal(barrier, inc=1, device_id=device, device_id_type=MESH)

    loop(A - 1, lambda k: greet(plane(lax.rem(ma + k + 1, A))))
    for h in range(H):
        loop(Z - 1, lambda k: greet(holder(h, lax.rem(zo + k + 1, Z))))

    def remote(src, dst, ssem, rsem, device):
        return pltpu.make_async_remote_copy(
            src_ref=src, dst_ref=dst, send_sem=ssem, recv_sem=rsem,
            device_id=device, device_id_type=MESH)

    recvs = (rb_ref, rc_ref, rf)

    def across(h):
        return (H - h) % H

    def tab_copy(h, k):
        z = lax.rem(zo + k, Z)
        return remote(tab_ref.at[h * Z + z], tabs.at[across(h) * Z + zo],
                      tab_s.at[h, k], tab_r.at[h, k], holder(h, z))

    def line_copy(s, side, r):
        z = zo - r if side else zo + r
        return remote(gath.at[s, z], gath.at[s, z], gath_s.at[s, side, r], gath_r.at[s, z],
                      holder(0, zo + 1 if side else zo - 1))

    def along(s, r, act):
        @pl.when((zo + 1 < Z) & (zo - r >= 0))
        def _():
            act(line_copy(s, 1, r))

        @pl.when((zo >= 1) & (zo + r < Z))
        def _():
            act(line_copy(s, 0, r))

    def pair_copy(s, h, j):
        z = zq * J + lax.rem(zj + j, J)
        return remote(gath.at[s, h * Z + zo], gath.at[s, h * Z + zo], pair_s.at[s, h, j],
                      pair_r.at[s, h, j], holder(0, z))

    def pair_in(s, h, j):
        z = zq * J + lax.rem(zj + J - j, J)
        return remote(gath.at[s, h * Z + z], gath.at[s, h * Z + z], pair_s.at[s, h, j],
                      pair_r.at[s, h, j], holder(0, z))

    def dense_copy(s, h, z):
        return remote(gath.at[s, z], gath.at[s, across(h) * Z + z],
                      dense_s.at[s, h, z], dense_r.at[s, h, z], holder(h, zo))

    for load in loads:
        load.wait()
    pl.semaphore_wait(barrier, A - 1 + H * (Z - 1))
    for s in (2, 0, 1):
        for h in range(1, H):
            dense_copy(s, h, zo).start()
    along(2, 0, lambda copy: copy.start())
    load_in.start()
    load_down.start()

    row = lax.broadcasted_iota(jnp.int32, (H * Z * D, JT), 0)
    h_of, z_of, t_of = row // (Z * D), (row // D) % Z, row % D
    g_of = (t_of // L) * sp + ((dc + h_of) % H) * sd
    expert = (g_of * inner + z_of * L + t_of % L).astype(F32)
    mine = lax.broadcasted_iota(jnp.int32, (1, JT), 1) // T == zj
    earlier = (lax.broadcasted_iota(jnp.int32, (JT, JT), 0)
               < lax.broadcasted_iota(jnp.int32, (JT, JT), 1)).astype(F32).astype(BF)
    tab_ref[...] = jnp.zeros_like(tab_ref)
    for which in range(2):
        ids = jnp.where(mine, jnp.concatenate([id_ref[which].astype(F32)] * J, axis=1), -1.0)
        scores = jnp.concatenate([sc_ref[which]] * J, axis=1)
        weights = scores / jnp.sum(scores, axis=0, keepdims=True)
        named = jnp.zeros((H * Z * D, JT), F32)
        weight = jnp.zeros((H * Z * D, JT), F32)
        for k in range(ids.shape[0]):
            hit = jnp.broadcast_to(ids[k:k + 1], (H * Z * D, JT)) == expert
            named = named + hit.astype(F32)
            weight = weight + jnp.where(hit, jnp.broadcast_to(weights[k:k + 1], (H * Z * D, JT)), 0.0)
        slot = jnp.where(named > 0.5, mm(named.astype(BF), earlier), -1.0)
        for b in range(H * Z):
            tab_ref[b, 2 * which * D:(2 * which + 1) * D, :JT] = slot[b * D:(b + 1) * D]
            tab_ref[b, (2 * which + 1) * D:(2 * which + 2) * D, :JT] = weight[b * D:(b + 1) * D]

    loop(Z - 1, lambda k: tab_copy(0, k + 1).start())
    for h in range(1, H):
        loop(Z, lambda k: tab_copy(h, k).start())
    tabs[zo] = tab_ref[zo]

    def hot(b, which):
        slots = [tabs[b * J + j, which * 2 * D:(which * 2 + 1) * D, :JT] for j in range(J)]
        want = lax.broadcasted_iota(jnp.int32, (C, JT), 0).astype(F32)
        return jnp.concatenate(
            [(jnp.broadcast_to(slots[j][t:t + 1], (C, JT)) == want).astype(F32)
             for t in range(D) for j in range(J)], axis=0)

    def weighted(b, which):
        w = [tabs[b * J + j, (which * 2 + 1) * D:(which * 2 + 2) * D, :JT] for j in range(J)]
        spread = jnp.concatenate(
            [jnp.broadcast_to(w[j][t:t + 1], (C, JT)) for t in range(D) for j in range(J)], axis=0)
        return hot(b, which) * spread

    def halves(full):
        high = full.astype(BF)
        return high, (full - high.astype(F32)).astype(BF)

    def rows_at(ref, index):
        return ref.at[pl.ds(pl.multiple_of(index * JC, 16), JC)]

    def place(e, b):
        return b * D + e

    def disp_copy(s, b, k):
        t = lax.rem(me + k, D)
        return remote(rows_at(send.at[s], b * D + t), rows_at(recvs[s], place(own, b)),
                      disp_s.at[s, b * D + t], disp_r.at[s, place(own, b)], target(t))

    def disp_in(s, b, k):
        at = place(lax.rem(own + k, D), b)
        return remote(rows_at(send.at[s], 0), rows_at(recvs[s], at),
                      disp_s.at[s, 0], disp_r.at[s, at], target(lax.rem(me + k, D)))

    def own_copy(s, b):
        return pltpu.make_async_copy(
            rows_at(send.at[s], b * D + me), rows_at(recvs[s], place(own, b)), own_sem.at[s, b])

    def span(index, size):
        return pl.ds(pl.multiple_of(index * size, size), size)

    tp = tile_of(width, 512)

    def pack(s, h, zp):
        b, q = zp * H + h, h * ZP + zp
        at = span(b, DC)
        pick = hot(q, 0 if s == 2 else 1).astype(BF)
        factor = jnp.sum(weighted(q, 1), axis=1, keepdims=True) if s == 1 else None

        def one(c):
            cols = span(c, tp)
            total = mm(pick, gath[s, pl.ds(q * J, J), :, cols].reshape(JT, tp))
            if s == 1:
                total = total * factor
            send[s, at, cols] = total.astype(BF)

        loop(width // tp, one)
        loop(D - 1, lambda k: disp_copy(s, b, k + 1).start())
        own_copy(s, b).start()

    def landed(s, r):
        for side in range(2):
            @pl.when((zo - r >= 0) if side else (zo + r < Z))
            def _():
                z = zo - r if side else zo + r
                line_copy(s, side, r).wait_recv()

                @pl.when(z // J != zq)
                def _():
                    for h in range(1, H):
                        dense_copy(s, h, z).start()

                if s == 2:
                    tab_copy(0, lax.rem(zo + Z - z, Z)).wait()

    def onward(s, r):
        along(s, r, lambda copy: copy.start())

    def direct(s, m):
        pack(s, 0, lax.rem(zq + ZP - m, ZP))

    def swap(s):
        for h in range(1, H):
            dense_copy(s, across(h), zo).wait_recv()
            for j in range(1, J):
                pair_copy(s, h, j).start()

    def relay(s, m):
        zp = lax.rem(zq + ZP - m, ZP)
        for h in range(1, H):
            for j in range(J):
                z = zp * J + j
                if s == 2:
                    tab_copy(across(h), lax.rem(zo + Z - z, Z)).wait()
                if not isinstance(m, int) or m > 0:
                    dense_copy(s, across(h), z).wait_recv()
                elif j > 0:
                    pair_in(s, h, j).wait_recv()
            pack(s, h, zp)

    def dense_sent(s):
        for h in range(1, H):
            def one(z, h=h):
                @pl.when((z == zo) | (z // J != zq))
                def _():
                    dense_copy(s, h, z).wait_send()

            loop(Z, one)
            for j in range(1, J):
                pair_copy(s, h, j).wait_send()

    def arrive(s, m):
        zp = lax.rem(zq + ZP - m, ZP)

        def one(h):
            b = zp * H + h
            loop(D - 1, lambda k: disp_in(s, b, k + 1).wait_recv())
            loop(D - 1, lambda k: disp_copy(s, b, k + 1).wait_send())
            own_copy(s, b).wait()

        loop(H, one)
        if s > 0:
            loop(D - 1, lambda k: pl.semaphore_signal(
                free.at[s - 1, m], inc=1, device_id=target(lax.rem(me + k + 1, D)), device_id_type=MESH))

    tf = tile_of(ff, 256)
    tw = tile_of(width, 256)
    chunk = H * D * JC
    results = (rf, send.at[0])
    backs = (send.at[2], send.at[1])

    def ret_copy(s, b, k):
        e = lax.rem(own + k, D)
        l = e // H
        p, d, step_p, step_d = axes_of(l)
        at = b * D + p * L + low
        return remote(rows_at(results[s], place(e, b)), rows_at(backs[s], at),
                      ret_s.at[s, place(e, b)], ret_r.at[s, at],
                      (lax.rem(e, H) * step_p + d * step_d, zo * L + l))

    def ret_in(s, b, k):
        t = lax.rem(me + k, D)
        return remote(rows_at(results[s], 0), rows_at(backs[s], b * D + t),
                      ret_s.at[s, 0], ret_r.at[s, b * D + t], target(t))

    def own_back(s, b):
        return pltpu.make_async_copy(
            rows_at(results[s], place(own, b)), rows_at(backs[s], b * D + me), own_sem.at[3 + s, b])

    def give_back(s, m):
        zp = lax.rem(zq + ZP - m, ZP)
        pl.semaphore_wait(free.at[1 - s, m], D - 1)

        def one(n):
            b = zp * H + lax.rem(n + 1, H)
            loop(D - 1, lambda k: ret_copy(s, b, k + 1).start())
            own_back(s, b).start()

        loop(H, one)

    def bwd_rows(m):
        at = span(lax.rem(zq + ZP - m, ZP), chunk)

        def hidden_tile(j):
            cols = span(j, tf)
            ups = pl.ds(pl.multiple_of(ff + j * tf, 128), tf)
            gate = mm(rb_ref[at], win_ref[:, cols])
            up = mm(rb_ref[at], win_ref[:, ups])
            d_hid = mm_cols(rc_ref[at], wdn_ref[cols])
            sig = jax.nn.sigmoid(gate)
            hid_ref[at, cols] = (gate * sig * up).astype(BF)
            dpr_ref[at, cols] = (d_hid * up * sig * (1.0 + gate * (1.0 - sig))).astype(BF)
            dpr_ref[at, ups] = (d_hid * gate * sig).astype(BF)

        loop(ff // tf, hidden_tile)

        def grad_tile(j):
            cols = span(j, tw)
            results[1][at, cols] = mm_cols(dpr_ref[at], win_ref[cols]).astype(BF)

        loop(width // tw, grad_tile)


    def fwd_rows(m):
        at = span(lax.rem(zq + ZP - m, ZP), chunk)

        def hidden_tile(j):
            cols = span(j, tf)
            gate = mm(rf[at], win_ref[:, cols])
            up = mm(rf[at], win_ref[:, pl.ds(pl.multiple_of(ff + j * tf, 128), tf)])
            stage[pl.ds(0, chunk), cols] = (gate * jax.nn.sigmoid(gate) * up).astype(BF)

        loop(ff // tf, hidden_tile)

        def out_tile(j):
            cols = span(j, tw)
            rf[at, cols] = mm(stage[pl.ds(0, chunk), pl.ds(0, ff)], wdn_ref[:, cols]).astype(BF)

        loop(width // tw, out_tile)

    def near_copy(s, h, zp):
        return remote(gath.at[s, pl.ds((h * ZP + zp) * J, J)],
                      near.at[s, pl.ds(((across(h) - 1) * ZP + zp) * J, J)],
                      near_s.at[s, h, zp], near_r.at[s, h, zp], holder(h, zo))

    def gathered(s, h, zp, sides=()):
        b, q = zp * H + h, h * ZP + zp
        loop(D - 1, lambda k: ret_in(s, b, k + 1).wait_recv())
        own_back(s, b).wait()
        for wait, _ in sides:
            wait()
        at = span(b, DC)
        picks = halves(weighted(q, 0)) if s == 0 else (hot(q, 1).astype(BF),)

        def one(c):
            cols = span(c, tp)
            value = backs[s][at, cols]
            total = mm_rows(picks[0], value)
            for more in picks[1:]:
                total = total + mm_rows(more, value)
            for _, first in sides:
                total = total + near[s, pl.ds(first, J), :, cols].reshape(JT, tp).astype(F32)
            gath[s, pl.ds(q * J, J), :, cols] = total.astype(BF).reshape(J, T, tp)

        loop(width // tp, one)

    def half_way(s, m):
        zp = lax.rem(zq + ZP - m, ZP)
        for h in range(1, H):
            gathered(s, h, zp)
            near_copy(s, h, zp).start()

    def part_copy(s, k):
        z = lax.rem(zo + k, Z)
        return remote(gath.at[s, z], parts.at[s, zo], part_s.at[s, k], part_r.at[s, k], holder(0, z))

    def settle(s):
        dense_sent(s)
        for r in range(Z - 1):
            along(s, r, lambda copy: copy.wait_send())

    def combine(s, m):
        zp = lax.rem(zq + ZP - m, ZP)
        gathered(s, 0, zp, [(near_copy(s, across(h), zp).wait_recv, ((h - 1) * ZP + zp) * J)
                            for h in range(1, H)])
        for j in range(0 if m else 1, J):
            part_copy(s, lax.rem(zp * J + lax.rem(zj + j, J) + Z - zo, Z)).start()
        if m == 0:
            parts[s, zo] = gath[s, zo]

    tg = math.gcd(tf, tw)
    count_in, count_down = width // tg, ff // tg

    def in_copy(j):
        slot = lax.rem(j, 2)
        return pltpu.make_async_copy(
            stage.at[span(slot, tg), pl.ds(0, 2 * ff)], gin_hbm.at[span(j, tg)], stage_sem.at[slot])

    def down_copy(j):
        slot = lax.rem(j, 2)
        return pltpu.make_async_copy(
            stage.at[span(slot, tg), pl.ds(0, width)], gdn_hbm.at[span(j, tg)], stage_sem.at[slot])

    def in_tile(j):
        value = mm_rows(rb_ref[:, span(j, tg)], dpr_ref[...]).astype(BF)

        @pl.when(j >= 2)
        def _():
            in_copy(j - 2).wait()

        stage[span(lax.rem(j, 2), tg), pl.ds(0, 2 * ff)] = value
        in_copy(j).start()

    def finish_in():
        for j in range(max(0, count_in - 2), count_in):
            in_copy(j).wait()

    def down_tile(j):
        value = mm_rows(hid_ref[:, span(j, tg)], rc_ref[...]).astype(BF)

        @pl.when(j >= 2)
        def _():
            down_copy(j - 2).wait()

        stage[span(lax.rem(j, 2), tg), pl.ds(0, width)] = value
        down_copy(j).start()

    far = range(1, ZP)
    order = (2, 0, 1)
    for p, s in enumerate(order):
        landed(s, 1)
        swap(s)
        if p < 2:
            onward(order[p + 1], 0)
        else:
            onward(order[0], 1)
        direct(s, 0)
        if p > 0:
            relay(order[p - 1], 0)
    relay(order[2], 0)
    for p, s in enumerate(order):
        landed(s, 2)
        onward(s, 2)
        if p < 2:
            onward(order[p + 1], 1)
        for r in range(3, Z):
            landed(s, r)
            onward(s, r)
        for m in far:
            direct(s, m)
        if p > 0:
            for m in far:
                relay(order[p - 1], m)
        if p == 1:
            arrive(2, 0)
            load_in.wait()
            load_down.wait()
            fwd_rows(0)
    for m in far:
        arrive(2, m)
        fwd_rows(m)
        give_back(0, m)
    for m in far:
        relay(1, m)
    arrive(0, 0)
    arrive(1, 0)
    bwd_rows(0)
    give_back(0, 0)
    for m in far:
        half_way(0, m)
    for m in far:
        arrive(0, m)
        arrive(1, m)
        bwd_rows(m)
        give_back(1, m)
    settle(0)
    settle(1)
    for m in far:
        combine(0, m)
    loop(count_down, down_tile)
    for j in range(max(0, count_down - 2), count_down):
        down_copy(j).wait()
    for m in far:
        half_way(1, m)
    give_back(1, 0)
    half_way(0, 0)
    for m in far:
        combine(1, m)
    combine(0, 0)
    half_way(1, 0)
    loop(count_in, in_tile)
    finish_in()
    combine(1, 0)
    outs = [pltpu.make_async_copy(out_ref.at[s], out, load_sem.at[s]) for s, out in enumerate((of_hbm, gt_hbm))]
    for s in (0, 1):
        loop(Z - 1, lambda k: part_copy(s, k + 1).wait())
        total = parts[s, 0].astype(F32)
        for z in range(1, Z):
            total = total + parts[s, z].astype(F32)
        out_ref[s] = total.astype(BF)
        outs[s].start()
    for r in range(Z - 1):
        along(2, r, lambda copy: copy.wait_send())
    for s in range(2):
        def sent(b, s=s):
            loop(D - 1, lambda k: ret_copy(s, b, k + 1).wait_send())

        loop(B, sent)
        for h in range(1, H):
            loop(ZP, lambda zp: near_copy(s, h, zp).wait_send())
    dense_sent(2)
    for out in outs:
        out.wait()


def hand_over(*refs):
    sources, targets, (held_in, held_down, held_tok, in_sem, out_sem) = refs[:4], refs[4:8], refs[8:]
    helds = (held_tok.at[0], held_tok.at[1], held_in, held_down)
    moves = []
    for n, (src, held, dst) in enumerate(zip(sources, helds, targets)):
        pieces = PIECES if src.shape[0] % (16 * PIECES) == 0 else 1
        size = src.shape[0] // pieces
        for p in range(pieces):
            at = pl.ds(p * size, size)
            moves.append((pltpu.make_async_copy(src.at[at], held.at[at], in_sem.at[n, p]),
                          pltpu.make_async_copy(held.at[at], dst.at[at], out_sem.at[n, p])))
    for load, _ in moves:
        load.start()
    for load, store in moves:
        load.wait()
        store.start()
    for _, store in moves:
        store.wait()


def shards(tokens_fwd, experts_fwd, scores_fwd, tokens_bwd, experts_bwd, scores_bwd,
           cotangent, w_in, w_down):
    G, inner = lax.axis_size("group"), lax.axis_size("inner")
    n = G * inner
    T, top = experts_fwd.shape
    width = tokens_fwd.shape[1]
    ff = w_down.shape[1]
    capacity = max(2, 3 * T * top // (2 * n))
    C = -(-capacity // 8) * 8
    Z = max(d for d in range(1, inner + 1) if inner % d == 0 and d * d <= n)
    L = inner // Z
    H = math.isqrt(G)
    assert H * H == G
    D = H * L
    rows = n * C
    J = 2
    assert Z % J == 0
    lanes = -(-J * T // 128) * 128
    dma = pltpu.SemaphoreType.DMA
    hbm = pl.BlockSpec(memory_space=pl.ANY)
    tg = math.gcd(tile_of(ff, 256), tile_of(width, 256))
    results = pl.pallas_call(
        functools.partial(layer_kernel, (Z, H, L, C, T, J, inner)),
        out_shape=(
            jax.ShapeDtypeStruct((T, width), BF),
            jax.ShapeDtypeStruct((T, width), BF),
            jax.ShapeDtypeStruct((width, 2 * ff), BF),
            jax.ShapeDtypeStruct((ff, width), BF),
        ),
        in_specs=[hbm] * 9,
        out_specs=(hbm,) * 4,
        scratch_shapes=[
            pltpu.VMEM((2, top, T), jnp.int32), pltpu.VMEM((2, top, T), F32),
            pltpu.VMEM((2, T, width), BF), dma((7,)),
            pltpu.VMEM((H * Z, 4 * D, lanes), F32),
            pltpu.VMEM((H * Z, 4 * D, lanes), F32),
            pltpu.VMEM((width, 2 * ff), BF),
            pltpu.VMEM((ff, width), BF),
            pltpu.VMEM((rows, width), BF),
            pltpu.VMEM((rows, width), BF),
            pltpu.VMEM((rows, width), BF),
            pltpu.VMEM((rows, ff), BF),
            pltpu.VMEM((rows, 2 * ff), BF),
            pltpu.VMEM((3, H * Z, T, width), BF),
            pltpu.VMEM((3, rows, width), BF),
            pltpu.VMEM((2, Z, T, width), BF),
            pltpu.VMEM((2, (H - 1) * Z, T, width), BF),
            pltpu.VMEM((2, (H - 1) * (J - 1), T, width), BF),
            pltpu.VMEM((max(2 * tg, rows // 2), max(2 * ff, width)), BF),
            dma((2,)),
            dma((5, H * Z)), dma((2,)), dma((H, Z)), dma((H, Z)), dma((3, 2, Z)), dma((3, Z)),
            dma((3, H, Z)), dma((3, H, Z)), dma((3, n)), dma((3, n)),
            dma((2, n)), dma((2, n)), dma((2, H, Z)), dma((2, H, Z)), dma((2, Z)), dma((2, Z)),
            dma((3, H, J)), dma((3, H, J)), dma((2, H * J)), dma((2, H * J)),
            pltpu.SemaphoreType.REGULAR((2, Z // J)),
        ],
        compiler_params=pltpu.CompilerParams(
            collective_id=0, has_side_effects=True, vmem_limit_bytes=67043328),
        name="moe_layer",
    )(experts_fwd.T, scores_fwd.T, experts_bwd.T, scores_bwd.T, tokens_bwd, cotangent, tokens_fwd, w_in[0], w_down[0])
    out_fwd, grad_tok, grad_in, grad_down = pl.pallas_call(
        hand_over,
        out_shape=tuple(jax.ShapeDtypeStruct(r.shape, r.dtype) for r in results),
        in_specs=[hbm] * 4,
        out_specs=(hbm,) * 4,
        scratch_shapes=[
            pltpu.VMEM((width, 2 * ff), BF), pltpu.VMEM((ff, width), BF), pltpu.VMEM((2, T, width), BF),
            dma((4, PIECES)), dma((4, PIECES)),
        ],
        compiler_params=pltpu.CompilerParams(vmem_limit_bytes=67043328),
        name="hand_over",
    )(*results)
    return out_fwd, grad_tok, grad_in[None], grad_down[None]


def solution(mesh):
    two, three = P(("group", "inner"), None), P(("group", "inner"), None, None)
    return jax.shard_map(
        shards, mesh=mesh,
        in_specs=(two,) * 7 + (three,) * 2,
        out_specs=(two, two, three, three),
        check_vma=False,
    )
```

```python
import functools
import math

import jax
import jax.numpy as jnp
from jax import lax
from jax.experimental import pallas as pl
from jax.experimental.pallas import tpu as pltpu
from jax.sharding import PartitionSpec as P

MESH = pl.DeviceIdType.MESH
BF = jnp.bfloat16
F32 = jnp.float32
PIECES = 8
ROWS = (((0,), (0,)), ((), ()))
COLS = (((1,), (1,)), ((), ()))


def mm(a, b):
    return jnp.dot(a, b, preferred_element_type=F32)


def mm_rows(a, b):
    return lax.dot_general(a, b, ROWS, preferred_element_type=F32)


def mm_cols(a, b):
    return lax.dot_general(a, b, COLS, preferred_element_type=F32)


def tile_of(size, most):
    return max(t for t in range(128, most + 1, 128) if size % t == 0)


def loop(count, body):
    lax.fori_loop(0, count, lambda k, c: (body(k), c)[1], 0)


def layer_kernel(dims, idf_hbm, scf_hbm, idb_hbm, scb_hbm, xb_hbm, ct_hbm, xf_hbm, win_hbm, wdn_hbm,
                 of_hbm, gt_hbm, gin_hbm, gdn_hbm, id_ref, sc_ref, out_ref, load_sem,
                 tab_ref, tabs, win_ref, wdn_ref, rb_ref, rc_ref, rf, hid_ref, dpr_ref,
                 gath, send, parts, near, mate, stage, stage_sem, own_sem, w_sem,
                 tab_s, tab_r, gath_s, gath_r, dense_s, dense_r, disp_s, disp_r,
                 ret_s, ret_r, near_s, near_r, part_s, part_r, pair_s, pair_r, mate_s, mate_r, free):
    Z, H, L, C, T, J, inner = dims
    D = H * L
    ZP, JC, JT = Z // J, J * C, J * T
    B = H * ZP
    DC = D * JC
    ff, width = wdn_ref.shape
    load_in = pltpu.make_async_copy(win_hbm, win_ref, w_sem.at[0])
    load_down = pltpu.make_async_copy(wdn_hbm, wdn_ref, w_sem.at[1])
    g = lax.axis_index("group")
    i = lax.axis_index("inner")
    zo, low = i // L, lax.rem(i, L)
    zq, zj = zo // J, lax.rem(zo, J)
    first, second = g // H, lax.rem(g, H)

    def axes_of(l):
        odd = lax.rem(l, 2)
        pack = first * (1 - odd) + second * odd
        dense = second * (1 - odd) + first * odd
        return pack, dense, H - odd * (H - 1), 1 + odd * (H - 1)

    pc, dc, sp, sd = axes_of(low)
    me = pc * L + low
    own = low * H + pc
    A = H * D
    ma = g * L + low

    def plane(a):
        return (a // L, zo * L + lax.rem(a, L))

    def holder(h, z):
        return (pc * sp + lax.rem(dc + h, H) * sd, z * L + low)

    def target(t):
        return ((t // L) * sp + dc * sd, zo * L + lax.rem(t, L))

    loads = [pltpu.make_async_copy(src, dst, load_sem.at[n]) for n, (src, dst) in enumerate((
        (xb_hbm, gath.at[0, zo]), (ct_hbm, gath.at[1, zo]), (xf_hbm, gath.at[2, zo]),
        (idf_hbm, id_ref.at[0]), (scf_hbm, sc_ref.at[0]),
        (idb_hbm, id_ref.at[1]), (scb_hbm, sc_ref.at[1])))]
    for load in loads:
        load.start()
    barrier = pltpu.get_barrier_semaphore()

    def greet(device):
        pl.semaphore_signal(barrier, inc=1, device_id=device, device_id_type=MESH)

    loop(A - 1, lambda k: greet(plane(lax.rem(ma + k + 1, A))))
    for h in range(H):
        loop(Z - 1, lambda k: greet(holder(h, lax.rem(zo + k + 1, Z))))

    def remote(src, dst, ssem, rsem, device):
        return pltpu.make_async_remote_copy(
            src_ref=src, dst_ref=dst, send_sem=ssem, recv_sem=rsem,
            device_id=device, device_id_type=MESH)

    recvs = (rb_ref, rc_ref, rf)

    def across(h):
        return (H - h) % H

    def tab_copy(h, k):
        z = lax.rem(zo + k, Z)
        return remote(tab_ref.at[h * Z + z], tabs.at[across(h) * Z + zo],
                      tab_s.at[h, k], tab_r.at[h, k], holder(h, z))

    def line_copy(s, side, r):
        z = zo - r if side else zo + r
        return remote(gath.at[s, z], gath.at[s, z], gath_s.at[s, side, r], gath_r.at[s, z],
                      holder(0, zo + 1 if side else zo - 1))

    def along(s, r, act):
        @pl.when((zo + 1 < Z) & (zo - r >= 0))
        def _():
            act(line_copy(s, 1, r))

        @pl.when((zo >= 1) & (zo + r < Z))
        def _():
            act(line_copy(s, 0, r))

    def pair_copy(s, h, j):
        z = zq * J + lax.rem(zj + j, J)
        return remote(gath.at[s, h * Z + zo], gath.at[s, h * Z + zo], pair_s.at[s, h, j],
                      pair_r.at[s, h, j], holder(0, z))

    def pair_in(s, h, j):
        z = zq * J + lax.rem(zj + J - j, J)
        return remote(gath.at[s, h * Z + z], gath.at[s, h * Z + z], pair_s.at[s, h, j],
                      pair_r.at[s, h, j], holder(0, z))

    def dense_copy(s, h, z):
        return remote(gath.at[s, z], gath.at[s, across(h) * Z + z],
                      dense_s.at[s, h, z], dense_r.at[s, h, z], holder(h, zo))

    for load in loads:
        load.wait()
    pl.semaphore_wait(barrier, A - 1 + H * (Z - 1))
    for s in (2, 0, 1):
        for h in range(1, H):
            dense_copy(s, h, zo).start()
    along(2, 0, lambda copy: copy.start())
    load_in.start()
    load_down.start()

    row = lax.broadcasted_iota(jnp.int32, (H * Z * D, JT), 0)
    h_of, z_of, t_of = row // (Z * D), (row // D) % Z, row % D
    g_of = (t_of // L) * sp + ((dc + h_of) % H) * sd
    expert = (g_of * inner + z_of * L + t_of % L).astype(F32)
    mine = lax.broadcasted_iota(jnp.int32, (1, JT), 1) // T == zj
    earlier = (lax.broadcasted_iota(jnp.int32, (JT, JT), 0)
               < lax.broadcasted_iota(jnp.int32, (JT, JT), 1)).astype(F32).astype(BF)
    tab_ref[...] = jnp.zeros_like(tab_ref)
    for which in range(2):
        ids = jnp.where(mine, jnp.concatenate([id_ref[which].astype(F32)] * J, axis=1), -1.0)
        scores = jnp.concatenate([sc_ref[which]] * J, axis=1)
        weights = scores / jnp.sum(scores, axis=0, keepdims=True)
        named = jnp.zeros((H * Z * D, JT), F32)
        weight = jnp.zeros((H * Z * D, JT), F32)
        for k in range(ids.shape[0]):
            hit = jnp.broadcast_to(ids[k:k + 1], (H * Z * D, JT)) == expert
            named = named + hit.astype(F32)
            weight = weight + jnp.where(hit, jnp.broadcast_to(weights[k:k + 1], (H * Z * D, JT)), 0.0)
        slot = jnp.where(named > 0.5, mm(named.astype(BF), earlier), -1.0)
        for b in range(H * Z):
            tab_ref[b, 2 * which * D:(2 * which + 1) * D, :JT] = slot[b * D:(b + 1) * D]
            tab_ref[b, (2 * which + 1) * D:(2 * which + 2) * D, :JT] = weight[b * D:(b + 1) * D]

    loop(Z - 1, lambda k: tab_copy(0, k + 1).start())
    for h in range(1, H):
        loop(Z, lambda k: tab_copy(h, k).start())
    tabs[zo] = tab_ref[zo]

    def hot(b, which):
        slots = [tabs[b * J + j, which * 2 * D:(which * 2 + 1) * D, :JT] for j in range(J)]
        want = lax.broadcasted_iota(jnp.int32, (C, JT), 0).astype(F32)
        return jnp.concatenate(
            [(jnp.broadcast_to(slots[j][t:t + 1], (C, JT)) == want).astype(F32)
             for t in range(D) for j in range(J)], axis=0)

    def weighted(b, which):
        w = [tabs[b * J + j, (which * 2 + 1) * D:(which * 2 + 2) * D, :JT] for j in range(J)]
        spread = jnp.concatenate(
            [jnp.broadcast_to(w[j][t:t + 1], (C, JT)) for t in range(D) for j in range(J)], axis=0)
        return hot(b, which) * spread

    def halves(full):
        high = full.astype(BF)
        return high, (full - high.astype(F32)).astype(BF)

    def rows_at(ref, index):
        return ref.at[pl.ds(pl.multiple_of(index * JC, 16), JC)]

    def place(e, b):
        return b * D + e

    def disp_copy(s, b, k):
        t = lax.rem(me + k, D)
        return remote(rows_at(send.at[s], b * D + t), rows_at(recvs[s], place(own, b)),
                      disp_s.at[s, b * D + t], disp_r.at[s, place(own, b)], target(t))

    def disp_in(s, b, k):
        at = place(lax.rem(own + k, D), b)
        return remote(rows_at(send.at[s], 0), rows_at(recvs[s], at),
                      disp_s.at[s, 0], disp_r.at[s, at], target(lax.rem(me + k, D)))

    def own_copy(s, b):
        return pltpu.make_async_copy(
            rows_at(send.at[s], b * D + me), rows_at(recvs[s], place(own, b)), own_sem.at[s, b])

    def span(index, size):
        return pl.ds(pl.multiple_of(index * size, size), size)

    tp = tile_of(width, 512)

    def pack(s, h, zp):
        b, q = zp * H + h, h * ZP + zp
        at = span(b, DC)
        pick = hot(q, 0 if s == 2 else 1).astype(BF)
        factor = jnp.sum(weighted(q, 1), axis=1, keepdims=True) if s == 1 else None

        def one(c):
            cols = span(c, tp)
            total = mm(pick, gath[s, pl.ds(q * J, J), :, cols].reshape(JT, tp))
            if s == 1:
                total = total * factor
            send[s, at, cols] = total.astype(BF)

        loop(width // tp, one)
        loop(D - 1, lambda k: disp_copy(s, b, k + 1).start())
        own_copy(s, b).start()

    def landed(s, r):
        for side in range(2):
            @pl.when((zo - r >= 0) if side else (zo + r < Z))
            def _():
                z = zo - r if side else zo + r
                line_copy(s, side, r).wait_recv()

                @pl.when(z // J != zq)
                def _():
                    for h in range(1, H):
                        dense_copy(s, h, z).start()

                if s == 2:
                    tab_copy(0, lax.rem(zo + Z - z, Z)).wait()

    def onward(s, r):
        along(s, r, lambda copy: copy.start())

    def direct(s, m):
        pack(s, 0, lax.rem(zq + ZP - m, ZP))

    def swap(s):
        for h in range(1, H):
            dense_copy(s, across(h), zo).wait_recv()
            for j in range(1, J):
                pair_copy(s, h, j).start()

    def relay(s, m):
        zp = lax.rem(zq + ZP - m, ZP)
        for h in range(1, H):
            for j in range(J):
                z = zp * J + j
                if s == 2:
                    tab_copy(across(h), lax.rem(zo + Z - z, Z)).wait()
                if not isinstance(m, int) or m > 0:
                    dense_copy(s, across(h), z).wait_recv()
                elif j > 0:
                    pair_in(s, h, j).wait_recv()
            pack(s, h, zp)

    def dense_sent(s):
        for h in range(1, H):
            def one(z, h=h):
                @pl.when((z == zo) | (z // J != zq))
                def _():
                    dense_copy(s, h, z).wait_send()

            loop(Z, one)
            for j in range(1, J):
                pair_copy(s, h, j).wait_send()

    def arrive(s, m):
        zp = lax.rem(zq + ZP - m, ZP)

        def one(h):
            b = zp * H + h
            loop(D - 1, lambda k: disp_in(s, b, k + 1).wait_recv())
            loop(D - 1, lambda k: disp_copy(s, b, k + 1).wait_send())
            own_copy(s, b).wait()

        loop(H, one)
        if s > 0:
            loop(D - 1, lambda k: pl.semaphore_signal(
                free.at[s - 1, m], inc=1, device_id=target(lax.rem(me + k + 1, D)), device_id_type=MESH))

    tf = tile_of(ff, 256)
    tw = tile_of(width, 256)
    chunk = H * D * JC
    results = (rf, send.at[0])
    backs = (send.at[2], send.at[1])

    def ret_copy(s, b, k):
        e = lax.rem(own + k, D)
        l = e // H
        p, d, step_p, step_d = axes_of(l)
        at = b * D + p * L + low
        return remote(rows_at(results[s], place(e, b)), rows_at(backs[s], at),
                      ret_s.at[s, place(e, b)], ret_r.at[s, at],
                      (lax.rem(e, H) * step_p + d * step_d, zo * L + l))

    def ret_in(s, b, k):
        t = lax.rem(me + k, D)
        return remote(rows_at(results[s], 0), rows_at(backs[s], b * D + t),
                      ret_s.at[s, 0], ret_r.at[s, b * D + t], target(t))

    def own_back(s, b):
        return pltpu.make_async_copy(
            rows_at(results[s], place(own, b)), rows_at(backs[s], b * D + me), own_sem.at[3 + s, b])

    def give_back(s, m):
        zp = lax.rem(zq + ZP - m, ZP)
        pl.semaphore_wait(free.at[1 - s, m], D - 1)

        def one(n):
            b = zp * H + lax.rem(n + 1, H)
            loop(D - 1, lambda k: ret_copy(s, b, k + 1).start())
            own_back(s, b).start()

        loop(H, one)

    def bwd_rows(m):
        at = span(lax.rem(zq + ZP - m, ZP), chunk)

        def hidden_tile(j):
            cols = span(j, tf)
            ups = pl.ds(pl.multiple_of(ff + j * tf, 128), tf)
            gate = mm(rb_ref[at], win_ref[:, cols])
            up = mm(rb_ref[at], win_ref[:, ups])
            d_hid = mm_cols(rc_ref[at], wdn_ref[cols])
            sig = jax.nn.sigmoid(gate)
            hid_ref[at, cols] = (gate * sig * up).astype(BF)
            dpr_ref[at, cols] = (d_hid * up * sig * (1.0 + gate * (1.0 - sig))).astype(BF)
            dpr_ref[at, ups] = (d_hid * gate * sig).astype(BF)

        loop(ff // tf, hidden_tile)

        def grad_tile(j):
            cols = span(j, tw)
            results[1][at, cols] = mm_cols(dpr_ref[at], win_ref[cols]).astype(BF)

        loop(width // tw, grad_tile)


    def fwd_rows(m):
        at = span(lax.rem(zq + ZP - m, ZP), chunk)

        def hidden_tile(j):
            cols = span(j, tf)
            gate = mm(rf[at], win_ref[:, cols])
            up = mm(rf[at], win_ref[:, pl.ds(pl.multiple_of(ff + j * tf, 128), tf)])
            stage[pl.ds(0, chunk), cols] = (gate * jax.nn.sigmoid(gate) * up).astype(BF)

        loop(ff // tf, hidden_tile)

        def out_tile(j):
            cols = span(j, tw)
            rf[at, cols] = mm(stage[pl.ds(0, chunk), pl.ds(0, ff)], wdn_ref[:, cols]).astype(BF)

        loop(width // tw, out_tile)

    def near_copy(s, h, zp):
        return remote(gath.at[s, pl.ds((h * ZP + zp) * J, J)],
                      near.at[s, pl.ds(((across(h) - 1) * ZP + zp) * J, J)],
                      near_s.at[s, h, zp], near_r.at[s, h, zp], holder(h, zo))

    def gathered(s, h, zp, sides=()):
        b, q = zp * H + h, h * ZP + zp
        loop(D - 1, lambda k: ret_in(s, b, k + 1).wait_recv())
        own_back(s, b).wait()
        for wait, _ in sides:
            wait()
        at = span(b, DC)
        picks = halves(weighted(q, 0)) if s == 0 else (hot(q, 1).astype(BF),)

        def one(c):
            cols = span(c, tp)
            value = backs[s][at, cols]
            total = mm_rows(picks[0], value)
            for more in picks[1:]:
                total = total + mm_rows(more, value)
            for _, first in sides:
                total = total + near[s, pl.ds(first, J), :, cols].reshape(JT, tp).astype(F32)
            gath[s, pl.ds(q * J, J), :, cols] = total.astype(BF).reshape(J, T, tp)

        loop(width // tp, one)

    def half_way(s, m):
        zp = lax.rem(zq + ZP - m, ZP)
        for h in range(1, H):
            gathered(s, h, zp)
            near_copy(s, h, zp).start()

    def part_copy(s, k):
        z = lax.rem(zo + k, Z)
        return remote(gath.at[s, z], parts.at[s, zo], part_s.at[s, k], part_r.at[s, k], holder(0, z))

    def settle(s):
        dense_sent(s)
        for r in range(Z - 1):
            along(s, r, lambda copy: copy.wait_send())

    def combine(s, m):
        zp = lax.rem(zq + ZP - m, ZP)
        gathered(s, 0, zp, [(near_copy(s, across(h), zp).wait_recv, ((h - 1) * ZP + zp) * J)
                            for h in range(1, H)])
        for j in range(0 if m else 1, J):
            part_copy(s, lax.rem(zp * J + lax.rem(zj + j, J) + Z - zo, Z)).start()
        if m == 0:
            parts[s, zo] = gath[s, zo]

    tg = math.gcd(tf, tw)
    count_in, count_down = width // tg, ff // tg

    def in_copy(j):
        slot = lax.rem(j, 2)
        return pltpu.make_async_copy(
            stage.at[span(slot, tg), pl.ds(0, 2 * ff)], gin_hbm.at[span(j, tg)], stage_sem.at[slot])

    def down_copy(j):
        slot = lax.rem(j, 2)
        return pltpu.make_async_copy(
            stage.at[span(slot, tg), pl.ds(0, width)], gdn_hbm.at[span(j, tg)], stage_sem.at[slot])

    def in_tile(j):
        value = mm_rows(rb_ref[:, span(j, tg)], dpr_ref[...]).astype(BF)

        @pl.when(j >= 2)
        def _():
            in_copy(j - 2).wait()

        stage[span(lax.rem(j, 2), tg), pl.ds(0, 2 * ff)] = value
        in_copy(j).start()

    def finish_in():
        for j in range(max(0, count_in - 2), count_in):
            in_copy(j).wait()

    def down_tile(j):
        value = mm_rows(hid_ref[:, span(j, tg)], rc_ref[...]).astype(BF)

        @pl.when(j >= 2)
        def _():
            down_copy(j - 2).wait()

        stage[span(lax.rem(j, 2), tg), pl.ds(0, width)] = value
        down_copy(j).start()

    far = range(1, ZP)
    order = (2, 0, 1)
    for p, s in enumerate(order):
        landed(s, 1)
        if p < 2:
            onward(order[p + 1], 0)
        else:
            onward(order[0], 1)
        direct(s, 0)
        swap(s)
        if p > 0:
            relay(order[p - 1], 0)
    relay(order[2], 0)
    for p, s in enumerate(order):
        landed(s, 2)
        onward(s, 2)
        if p < 2:
            onward(order[p + 1], 1)
        for r in range(3, Z):
            landed(s, r)
            onward(s, r)
        for m in far:
            direct(s, m)
        if p > 0:
            for m in far:
                relay(order[p - 1], m)
        if p == 1:
            arrive(2, 0)
            load_in.wait()
            load_down.wait()
            fwd_rows(0)
    for m in far:
        arrive(2, m)
        fwd_rows(m)
        give_back(0, m)
    for m in far:
        relay(1, m)
    arrive(0, 0)
    arrive(1, 0)
    bwd_rows(0)
    give_back(0, 0)
    for m in far:
        half_way(0, m)
    for m in far:
        arrive(0, m)
        arrive(1, m)
        bwd_rows(m)
        give_back(1, m)
    settle(0)
    settle(1)
    for m in far:
        combine(0, m)
    loop(count_down, down_tile)
    for j in range(max(0, count_down - 2), count_down):
        down_copy(j).wait()
    for m in far:
        half_way(1, m)
    give_back(1, 0)
    half_way(0, 0)
    for m in far:
        combine(1, m)
    combine(0, 0)
    half_way(1, 0)
    loop(count_in, in_tile)
    finish_in()
    combine(1, 0)
    outs = [pltpu.make_async_copy(out_ref.at[s], out, load_sem.at[s]) for s, out in enumerate((of_hbm, gt_hbm))]
    for s in (0, 1):
        loop(Z - 1, lambda k: part_copy(s, k + 1).wait())
        total = parts[s, 0].astype(F32)
        for z in range(1, Z):
            total = total + parts[s, z].astype(F32)
        out_ref[s] = total.astype(BF)
        outs[s].start()
    for r in range(Z - 1):
        along(2, r, lambda copy: copy.wait_send())
    for s in range(2):
        def sent(b, s=s):
            loop(D - 1, lambda k: ret_copy(s, b, k + 1).wait_send())

        loop(B, sent)
        for h in range(1, H):
            loop(ZP, lambda zp: near_copy(s, h, zp).wait_send())
    dense_sent(2)
    for out in outs:
        out.wait()


def hand_over(*refs):
    sources, targets, (held_in, held_down, held_tok, in_sem, out_sem) = refs[:4], refs[4:8], refs[8:]
    helds = (held_tok.at[0], held_tok.at[1], held_in, held_down)
    moves = []
    for n, (src, held, dst) in enumerate(zip(sources, helds, targets)):
        pieces = PIECES if src.shape[0] % (16 * PIECES) == 0 else 1
        size = src.shape[0] // pieces
        for p in range(pieces):
            at = pl.ds(p * size, size)
            moves.append((pltpu.make_async_copy(src.at[at], held.at[at], in_sem.at[n, p]),
                          pltpu.make_async_copy(held.at[at], dst.at[at], out_sem.at[n, p])))
    for load, _ in moves:
        load.start()
    for load, store in moves:
        load.wait()
        store.start()
    for _, store in moves:
        store.wait()


def shards(tokens_fwd, experts_fwd, scores_fwd, tokens_bwd, experts_bwd, scores_bwd,
           cotangent, w_in, w_down):
    G, inner = lax.axis_size("group"), lax.axis_size("inner")
    n = G * inner
    T, top = experts_fwd.shape
    width = tokens_fwd.shape[1]
    ff = w_down.shape[1]
    capacity = max(2, 3 * T * top // (2 * n))
    C = -(-capacity // 8) * 8
    Z = max(d for d in range(1, inner + 1) if inner % d == 0 and d * d <= n)
    L = inner // Z
    H = math.isqrt(G)
    assert H * H == G
    D = H * L
    rows = n * C
    J = 2
    assert Z % J == 0
    lanes = -(-J * T // 128) * 128
    dma = pltpu.SemaphoreType.DMA
    hbm = pl.BlockSpec(memory_space=pl.ANY)
    tg = math.gcd(tile_of(ff, 256), tile_of(width, 256))
    results = pl.pallas_call(
        functools.partial(layer_kernel, (Z, H, L, C, T, J, inner)),
        out_shape=(
            jax.ShapeDtypeStruct((T, width), BF),
            jax.ShapeDtypeStruct((T, width), BF),
            jax.ShapeDtypeStruct((width, 2 * ff), BF),
            jax.ShapeDtypeStruct((ff, width), BF),
        ),
        in_specs=[hbm] * 9,
        out_specs=(hbm,) * 4,
        scratch_shapes=[
            pltpu.VMEM((2, top, T), jnp.int32), pltpu.VMEM((2, top, T), F32),
            pltpu.VMEM((2, T, width), BF), dma((7,)),
            pltpu.VMEM((H * Z, 4 * D, lanes), F32),
            pltpu.VMEM((H * Z, 4 * D, lanes), F32),
            pltpu.VMEM((width, 2 * ff), BF),
            pltpu.VMEM((ff, width), BF),
            pltpu.VMEM((rows, width), BF),
            pltpu.VMEM((rows, width), BF),
            pltpu.VMEM((rows, width), BF),
            pltpu.VMEM((rows, ff), BF),
            pltpu.VMEM((rows, 2 * ff), BF),
            pltpu.VMEM((3, H * Z, T, width), BF),
            pltpu.VMEM((3, rows, width), BF),
            pltpu.VMEM((2, Z, T, width), BF),
            pltpu.VMEM((2, (H - 1) * Z, T, width), BF),
            pltpu.VMEM((2, (H - 1) * (J - 1), T, width), BF),
            pltpu.VMEM((max(2 * tg, rows // 2), max(2 * ff, width)), BF),
            dma((2,)),
            dma((5, H * Z)), dma((2,)), dma((H, Z)), dma((H, Z)), dma((3, 2, Z)), dma((3, Z)),
            dma((3, H, Z)), dma((3, H, Z)), dma((3, n)), dma((3, n)),
            dma((2, n)), dma((2, n)), dma((2, H, Z)), dma((2, H, Z)), dma((2, Z)), dma((2, Z)),
            dma((3, H, J)), dma((3, H, J)), dma((2, H * J)), dma((2, H * J)),
            pltpu.SemaphoreType.REGULAR((2, Z // J)),
        ],
        compiler_params=pltpu.CompilerParams(
            collective_id=0, has_side_effects=True, vmem_limit_bytes=67043328),
        name="moe_layer",
    )(experts_fwd.T, scores_fwd.T, experts_bwd.T, scores_bwd.T, tokens_bwd, cotangent, tokens_fwd, w_in[0], w_down[0])
    out_fwd, grad_tok, grad_in, grad_down = pl.pallas_call(
        hand_over,
        out_shape=tuple(jax.ShapeDtypeStruct(r.shape, r.dtype) for r in results),
        in_specs=[hbm] * 4,
        out_specs=(hbm,) * 4,
        scratch_shapes=[
            pltpu.VMEM((width, 2 * ff), BF), pltpu.VMEM((ff, width), BF), pltpu.VMEM((2, T, width), BF),
            dma((4, PIECES)), dma((4, PIECES)),
        ],
        compiler_params=pltpu.CompilerParams(vmem_limit_bytes=67043328),
        name="hand_over",
    )(*results)
    return out_fwd, grad_tok, grad_in[None], grad_down[None]


def solution(mesh):
    two, three = P(("group", "inner"), None), P(("group", "inner"), None, None)
    return jax.shard_map(
        shards, mesh=mesh,
        in_specs=(two,) * 7 + (three,) * 2,
        out_specs=(two, two, three, three),
        check_vma=False,
    )
```

```python
import functools
import math

import jax
import jax.numpy as jnp
from jax import lax
from jax.experimental import pallas as pl
from jax.experimental.pallas import tpu as pltpu
from jax.sharding import PartitionSpec as P

MESH = pl.DeviceIdType.MESH
BF = jnp.bfloat16
F32 = jnp.float32
PIECES = 8
ROWS = (((0,), (0,)), ((), ()))
COLS = (((1,), (1,)), ((), ()))


def mm(a, b):
    return jnp.dot(a, b, preferred_element_type=F32)


def mm_rows(a, b):
    return lax.dot_general(a, b, ROWS, preferred_element_type=F32)


def mm_cols(a, b):
    return lax.dot_general(a, b, COLS, preferred_element_type=F32)


def tile_of(size, most):
    return max(t for t in range(128, most + 1, 128) if size % t == 0)


def loop(count, body):
    lax.fori_loop(0, count, lambda k, c: (body(k), c)[1], 0)


def layer_kernel(dims, idf_hbm, scf_hbm, idb_hbm, scb_hbm, xb_hbm, ct_hbm, xf_hbm, win_hbm, wdn_hbm,
                 of_hbm, gt_hbm, gin_hbm, gdn_hbm, id_ref, sc_ref, out_ref, load_sem,
                 tab_ref, tabs, win_ref, wdn_ref, rb_ref, rc_ref, rf, hid_ref, dpr_ref,
                 gath, send, parts, near, mate, stage, stage_sem, own_sem, w_sem,
                 tab_s, tab_r, gath_s, gath_r, dense_s, dense_r, disp_s, disp_r,
                 ret_s, ret_r, near_s, near_r, part_s, part_r, pair_s, pair_r, mate_s, mate_r, free):
    Z, H, L, C, T, J, inner = dims
    D = H * L
    ZP, JC, JT = Z // J, J * C, J * T
    B = H * ZP
    DC = D * JC
    ff, width = wdn_ref.shape
    load_in = pltpu.make_async_copy(win_hbm, win_ref, w_sem.at[0])
    load_down = pltpu.make_async_copy(wdn_hbm, wdn_ref, w_sem.at[1])
    g = lax.axis_index("group")
    i = lax.axis_index("inner")
    zo, low = i // L, lax.rem(i, L)
    zq, zj = zo // J, lax.rem(zo, J)
    first, second = g // H, lax.rem(g, H)

    def axes_of(l):
        odd = lax.rem(l, 2)
        pack = first * (1 - odd) + second * odd
        dense = second * (1 - odd) + first * odd
        return pack, dense, H - odd * (H - 1), 1 + odd * (H - 1)

    pc, dc, sp, sd = axes_of(low)
    me = pc * L + low
    own = low * H + pc
    A = H * D
    ma = g * L + low

    def plane(a):
        return (a // L, zo * L + lax.rem(a, L))

    def holder(h, z):
        return (pc * sp + lax.rem(dc + h, H) * sd, z * L + low)

    def target(t):
        return ((t // L) * sp + dc * sd, zo * L + lax.rem(t, L))

    loads = [pltpu.make_async_copy(src, dst, load_sem.at[n]) for n, (src, dst) in enumerate((
        (xb_hbm, gath.at[0, zo]), (ct_hbm, gath.at[1, zo]), (xf_hbm, gath.at[2, zo]),
        (idf_hbm, id_ref.at[0]), (scf_hbm, sc_ref.at[0]),
        (idb_hbm, id_ref.at[1]), (scb_hbm, sc_ref.at[1])))]
    for load in loads:
        load.start()
    barrier = pltpu.get_barrier_semaphore()

    def greet(device):
        pl.semaphore_signal(barrier, inc=1, device_id=device, device_id_type=MESH)

    loop(A - 1, lambda k: greet(plane(lax.rem(ma + k + 1, A))))
    for h in range(H):
        loop(Z - 1, lambda k: greet(holder(h, lax.rem(zo + k + 1, Z))))

    def remote(src, dst, ssem, rsem, device):
        return pltpu.make_async_remote_copy(
            src_ref=src, dst_ref=dst, send_sem=ssem, recv_sem=rsem,
            device_id=device, device_id_type=MESH)

    recvs = (rb_ref, rc_ref, rf)

    def across(h):
        return (H - h) % H

    def tab_copy(h, k):
        z = lax.rem(zo + k, Z)
        return remote(tab_ref.at[h * Z + z], tabs.at[across(h) * Z + zo],
                      tab_s.at[h, k], tab_r.at[h, k], holder(h, z))

    def line_copy(s, side, r):
        z = zo - r if side else zo + r
        return remote(gath.at[s, z], gath.at[s, z], gath_s.at[s, side, r], gath_r.at[s, z],
                      holder(0, zo + 1 if side else zo - 1))

    def along(s, r, act):
        @pl.when((zo + 1 < Z) & (zo - r >= 0))
        def _():
            act(line_copy(s, 1, r))

        @pl.when((zo >= 1) & (zo + r < Z))
        def _():
            act(line_copy(s, 0, r))

    def pair_copy(s, h, j):
        z = zq * J + lax.rem(zj + j, J)
        return remote(gath.at[s, h * Z + zo], gath.at[s, h * Z + zo], pair_s.at[s, h, j],
                      pair_r.at[s, h, j], holder(0, z))

    def pair_in(s, h, j):
        z = zq * J + lax.rem(zj + J - j, J)
        return remote(gath.at[s, h * Z + z], gath.at[s, h * Z + z], pair_s.at[s, h, j],
                      pair_r.at[s, h, j], holder(0, z))

    def dense_copy(s, h, z):
        return remote(gath.at[s, z], gath.at[s, across(h) * Z + z],
                      dense_s.at[s, h, z], dense_r.at[s, h, z], holder(h, zo))

    for load in loads:
        load.wait()
    pl.semaphore_wait(barrier, A - 1 + H * (Z - 1))
    for h in range(1, H):
        dense_copy(2, h, zo).start()
    along(2, 0, lambda copy: copy.start())
    load_in.start()
    load_down.start()

    row = lax.broadcasted_iota(jnp.int32, (H * Z * D, JT), 0)
    h_of, z_of, t_of = row // (Z * D), (row // D) % Z, row % D
    g_of = (t_of // L) * sp + ((dc + h_of) % H) * sd
    expert = (g_of * inner + z_of * L + t_of % L).astype(F32)
    mine = lax.broadcasted_iota(jnp.int32, (1, JT), 1) // T == zj
    earlier = (lax.broadcasted_iota(jnp.int32, (JT, JT), 0)
               < lax.broadcasted_iota(jnp.int32, (JT, JT), 1)).astype(F32).astype(BF)
    tab_ref[...] = jnp.zeros_like(tab_ref)
    for which in range(2):
        ids = jnp.where(mine, jnp.concatenate([id_ref[which].astype(F32)] * J, axis=1), -1.0)
        scores = jnp.concatenate([sc_ref[which]] * J, axis=1)
        weights = scores / jnp.sum(scores, axis=0, keepdims=True)
        named = jnp.zeros((H * Z * D, JT), F32)
        weight = jnp.zeros((H * Z * D, JT), F32)
        for k in range(ids.shape[0]):
            hit = jnp.broadcast_to(ids[k:k + 1], (H * Z * D, JT)) == expert
            named = named + hit.astype(F32)
            weight = weight + jnp.where(hit, jnp.broadcast_to(weights[k:k + 1], (H * Z * D, JT)), 0.0)
        slot = jnp.where(named > 0.5, mm(named.astype(BF), earlier), -1.0)
        for b in range(H * Z):
            tab_ref[b, 2 * which * D:(2 * which + 1) * D, :JT] = slot[b * D:(b + 1) * D]
            tab_ref[b, (2 * which + 1) * D:(2 * which + 2) * D, :JT] = weight[b * D:(b + 1) * D]

    loop(Z - 1, lambda k: tab_copy(0, k + 1).start())
    for h in range(1, H):
        loop(Z, lambda k: tab_copy(h, k).start())
    tabs[zo] = tab_ref[zo]

    def hot(b, which):
        slots = [tabs[b * J + j, which * 2 * D:(which * 2 + 1) * D, :JT] for j in range(J)]
        want = lax.broadcasted_iota(jnp.int32, (C, JT), 0).astype(F32)
        return jnp.concatenate(
            [(jnp.broadcast_to(slots[j][t:t + 1], (C, JT)) == want).astype(F32)
             for t in range(D) for j in range(J)], axis=0)

    def weighted(b, which):
        w = [tabs[b * J + j, (which * 2 + 1) * D:(which * 2 + 2) * D, :JT] for j in range(J)]
        spread = jnp.concatenate(
            [jnp.broadcast_to(w[j][t:t + 1], (C, JT)) for t in range(D) for j in range(J)], axis=0)
        return hot(b, which) * spread

    def halves(full):
        high = full.astype(BF)
        return high, (full - high.astype(F32)).astype(BF)

    def rows_at(ref, index):
        return ref.at[pl.ds(pl.multiple_of(index * JC, 16), JC)]

    def place(e, b):
        return b * D + e

    def disp_copy(s, b, k):
        t = lax.rem(me + k, D)
        return remote(rows_at(send.at[s], b * D + t), rows_at(recvs[s], place(own, b)),
                      disp_s.at[s, b * D + t], disp_r.at[s, place(own, b)], target(t))

    def disp_in(s, b, k):
        at = place(lax.rem(own + k, D), b)
        return remote(rows_at(send.at[s], 0), rows_at(recvs[s], at),
                      disp_s.at[s, 0], disp_r.at[s, at], target(lax.rem(me + k, D)))

    def own_copy(s, b):
        return pltpu.make_async_copy(
            rows_at(send.at[s], b * D + me), rows_at(recvs[s], place(own, b)), own_sem.at[s, b])

    def span(index, size):
        return pl.ds(pl.multiple_of(index * size, size), size)

    tp = tile_of(width, 512)

    def pack(s, h, zp):
        b, q = zp * H + h, h * ZP + zp
        at = span(b, DC)
        pick = hot(q, 0 if s == 2 else 1).astype(BF)
        factor = jnp.sum(weighted(q, 1), axis=1, keepdims=True) if s == 1 else None

        def one(c):
            cols = span(c, tp)
            total = mm(pick, gath[s, pl.ds(q * J, J), :, cols].reshape(JT, tp))
            if s == 1:
                total = total * factor
            send[s, at, cols] = total.astype(BF)

        loop(width // tp, one)
        loop(D - 1, lambda k: disp_copy(s, b, k + 1).start())
        own_copy(s, b).start()

    def landed(s, r):
        for side in range(2):
            @pl.when((zo - r >= 0) if side else (zo + r < Z))
            def _():
                z = zo - r if side else zo + r
                line_copy(s, side, r).wait_recv()

                @pl.when(z // J != zq)
                def _():
                    for h in range(1, H):
                        dense_copy(s, h, z).start()

                if s == 2:
                    tab_copy(0, lax.rem(zo + Z - z, Z)).wait()

    def onward(s, r):
        along(s, r, lambda copy: copy.start())

    def direct(s, m):
        pack(s, 0, lax.rem(zq + ZP - m, ZP))

    def swap(s):
        for h in range(1, H):
            dense_copy(s, across(h), zo).wait_recv()
            for j in range(1, J):
                pair_copy(s, h, j).start()

    def relay(s, m):
        zp = lax.rem(zq + ZP - m, ZP)
        for h in range(1, H):
            for j in range(J):
                z = zp * J + j
                if s == 2:
                    tab_copy(across(h), lax.rem(zo + Z - z, Z)).wait()
                if not isinstance(m, int) or m > 0:
                    dense_copy(s, across(h), z).wait_recv()
                elif j > 0:
                    pair_in(s, h, j).wait_recv()
            pack(s, h, zp)

    def dense_sent(s):
        for h in range(1, H):
            def one(z, h=h):
                @pl.when((z == zo) | (z // J != zq))
                def _():
                    dense_copy(s, h, z).wait_send()

            loop(Z, one)
            for j in range(1, J):
                pair_copy(s, h, j).wait_send()

    def arrive(s, m):
        zp = lax.rem(zq + ZP - m, ZP)

        def one(h):
            b = zp * H + h
            loop(D - 1, lambda k: disp_in(s, b, k + 1).wait_recv())
            loop(D - 1, lambda k: disp_copy(s, b, k + 1).wait_send())
            own_copy(s, b).wait()

        loop(H, one)
        if s > 0:
            loop(D - 1, lambda k: pl.semaphore_signal(
                free.at[s - 1, m], inc=1, device_id=target(lax.rem(me + k + 1, D)), device_id_type=MESH))

    tf = tile_of(ff, 256)
    tw = tile_of(width, 256)
    chunk = H * D * JC
    results = (rf, send.at[0])
    backs = (send.at[2], send.at[1])

    def ret_copy(s, b, k):
        e = lax.rem(own + k, D)
        l = e // H
        p, d, step_p, step_d = axes_of(l)
        at = b * D + p * L + low
        return remote(rows_at(results[s], place(e, b)), rows_at(backs[s], at),
                      ret_s.at[s, place(e, b)], ret_r.at[s, at],
                      (lax.rem(e, H) * step_p + d * step_d, zo * L + l))

    def ret_in(s, b, k):
        t = lax.rem(me + k, D)
        return remote(rows_at(results[s], 0), rows_at(backs[s], b * D + t),
                      ret_s.at[s, 0], ret_r.at[s, b * D + t], target(t))

    def own_back(s, b):
        return pltpu.make_async_copy(
            rows_at(results[s], place(own, b)), rows_at(backs[s], b * D + me), own_sem.at[3 + s, b])

    def give_back(s, m):
        zp = lax.rem(zq + ZP - m, ZP)
        pl.semaphore_wait(free.at[1 - s, m], D - 1)

        def one(n):
            b = zp * H + lax.rem(n + 1, H)
            loop(D - 1, lambda k: ret_copy(s, b, k + 1).start())
            own_back(s, b).start()

        loop(H, one)

    def bwd_rows(m):
        at = span(lax.rem(zq + ZP - m, ZP), chunk)

        def hidden_tile(j):
            cols = span(j, tf)
            ups = pl.ds(pl.multiple_of(ff + j * tf, 128), tf)
            gate = mm(rb_ref[at], win_ref[:, cols])
            up = mm(rb_ref[at], win_ref[:, ups])
            d_hid = mm_cols(rc_ref[at], wdn_ref[cols])
            sig = jax.nn.sigmoid(gate)
            hid_ref[at, cols] = (gate * sig * up).astype(BF)
            dpr_ref[at, cols] = (d_hid * up * sig * (1.0 + gate * (1.0 - sig))).astype(BF)
            dpr_ref[at, ups] = (d_hid * gate * sig).astype(BF)

        loop(ff // tf, hidden_tile)

        def grad_tile(j):
            cols = span(j, tw)
            results[1][at, cols] = mm_cols(dpr_ref[at], win_ref[cols]).astype(BF)

        loop(width // tw, grad_tile)


    def fwd_rows(m):
        at = span(lax.rem(zq + ZP - m, ZP), chunk)

        def hidden_tile(j):
            cols = span(j, tf)
            gate = mm(rf[at], win_ref[:, cols])
            up = mm(rf[at], win_ref[:, pl.ds(pl.multiple_of(ff + j * tf, 128), tf)])
            stage[pl.ds(0, chunk), cols] = (gate * jax.nn.sigmoid(gate) * up).astype(BF)

        loop(ff // tf, hidden_tile)

        def out_tile(j):
            cols = span(j, tw)
            rf[at, cols] = mm(stage[pl.ds(0, chunk), pl.ds(0, ff)], wdn_ref[:, cols]).astype(BF)

        loop(width // tw, out_tile)

    def near_copy(s, h, zp):
        return remote(gath.at[s, pl.ds((h * ZP + zp) * J, J)],
                      near.at[s, pl.ds(((across(h) - 1) * ZP + zp) * J, J)],
                      near_s.at[s, h, zp], near_r.at[s, h, zp], holder(h, zo))

    def gathered(s, h, zp, sides=()):
        b, q = zp * H + h, h * ZP + zp
        loop(D - 1, lambda k: ret_in(s, b, k + 1).wait_recv())
        own_back(s, b).wait()
        for wait, _ in sides:
            wait()
        at = span(b, DC)
        picks = halves(weighted(q, 0)) if s == 0 else (hot(q, 1).astype(BF),)

        def one(c):
            cols = span(c, tp)
            value = backs[s][at, cols]
            total = mm_rows(picks[0], value)
            for more in picks[1:]:
                total = total + mm_rows(more, value)
            for _, first in sides:
                total = total + near[s, pl.ds(first, J), :, cols].reshape(JT, tp).astype(F32)
            gath[s, pl.ds(q * J, J), :, cols] = total.astype(BF).reshape(J, T, tp)

        loop(width // tp, one)

    def half_way(s, m):
        zp = lax.rem(zq + ZP - m, ZP)
        for h in range(1, H):
            gathered(s, h, zp)
            near_copy(s, h, zp).start()

    def part_copy(s, k):
        z = lax.rem(zo + k, Z)
        return remote(gath.at[s, z], parts.at[s, zo], part_s.at[s, k], part_r.at[s, k], holder(0, z))

    def settle(s):
        dense_sent(s)
        for r in range(Z - 1):
            along(s, r, lambda copy: copy.wait_send())

    def combine(s, m):
        zp = lax.rem(zq + ZP - m, ZP)
        gathered(s, 0, zp, [(near_copy(s, across(h), zp).wait_recv, ((h - 1) * ZP + zp) * J)
                            for h in range(1, H)])
        for j in range(0 if m else 1, J):
            part_copy(s, lax.rem(zp * J + lax.rem(zj + j, J) + Z - zo, Z)).start()
        if m == 0:
            parts[s, zo] = gath[s, zo]

    tg = math.gcd(tf, tw)
    count_in, count_down = width // tg, ff // tg

    def in_copy(j):
        slot = lax.rem(j, 2)
        return pltpu.make_async_copy(
            stage.at[span(slot, tg), pl.ds(0, 2 * ff)], gin_hbm.at[span(j, tg)], stage_sem.at[slot])

    def down_copy(j):
        slot = lax.rem(j, 2)
        return pltpu.make_async_copy(
            stage.at[span(slot, tg), pl.ds(0, width)], gdn_hbm.at[span(j, tg)], stage_sem.at[slot])

    def in_tile(j):
        value = mm_rows(rb_ref[:, span(j, tg)], dpr_ref[...]).astype(BF)

        @pl.when(j >= 2)
        def _():
            in_copy(j - 2).wait()

        stage[span(lax.rem(j, 2), tg), pl.ds(0, 2 * ff)] = value
        in_copy(j).start()

    def finish_in():
        for j in range(max(0, count_in - 2), count_in):
            in_copy(j).wait()

    def down_tile(j):
        value = mm_rows(hid_ref[:, span(j, tg)], rc_ref[...]).astype(BF)

        @pl.when(j >= 2)
        def _():
            down_copy(j - 2).wait()

        stage[span(lax.rem(j, 2), tg), pl.ds(0, width)] = value
        down_copy(j).start()

    far = range(1, ZP)
    order = (2, 0, 1)
    for p, s in enumerate(order):
        landed(s, 1)
        if p < 2:
            onward(order[p + 1], 0)
            for h in range(1, H):
                dense_copy(order[p + 1], h, zo).start()
        if p == 1:
            onward(order[0], 1)
        direct(s, 0)
        swap(s)
        if p > 0:
            relay(order[p - 1], 0)
    relay(order[2], 0)
    for p, s in enumerate(order):
        landed(s, 2)
        onward(s, 2)
        if p < 2:
            onward(order[p + 1], 1)
        for r in range(3, Z):
            landed(s, r)
            onward(s, r)
        for m in far:
            direct(s, m)
        if p > 0:
            for m in far:
                relay(order[p - 1], m)
        if p == 1:
            arrive(2, 0)
            load_in.wait()
            load_down.wait()
            fwd_rows(0)
    for m in far:
        arrive(2, m)
        fwd_rows(m)
        give_back(0, m)
    for m in far:
        relay(1, m)
    arrive(0, 0)
    arrive(1, 0)
    bwd_rows(0)
    give_back(0, 0)
    for m in far:
        half_way(0, m)
    for m in far:
        arrive(0, m)
        arrive(1, m)
        bwd_rows(m)
        give_back(1, m)
    settle(0)
    settle(1)
    for m in far:
        combine(0, m)
    loop(count_down, down_tile)
    for j in range(max(0, count_down - 2), count_down):
        down_copy(j).wait()
    for m in far:
        half_way(1, m)
    give_back(1, 0)
    half_way(0, 0)
    for m in far:
        combine(1, m)
    combine(0, 0)
    half_way(1, 0)
    loop(count_in, in_tile)
    finish_in()
    combine(1, 0)
    outs = [pltpu.make_async_copy(out_ref.at[s], out, load_sem.at[s]) for s, out in enumerate((of_hbm, gt_hbm))]
    for s in (0, 1):
        loop(Z - 1, lambda k: part_copy(s, k + 1).wait())
        total = parts[s, 0].astype(F32)
        for z in range(1, Z):
            total = total + parts[s, z].astype(F32)
        out_ref[s] = total.astype(BF)
        outs[s].start()
    for r in range(Z - 1):
        along(2, r, lambda copy: copy.wait_send())
    for s in range(2):
        def sent(b, s=s):
            loop(D - 1, lambda k: ret_copy(s, b, k + 1).wait_send())

        loop(B, sent)
        for h in range(1, H):
            loop(ZP, lambda zp: near_copy(s, h, zp).wait_send())
    dense_sent(2)
    for out in outs:
        out.wait()


def hand_over(*refs):
    sources, targets, (held_in, held_down, held_tok, in_sem, out_sem) = refs[:4], refs[4:8], refs[8:]
    helds = (held_tok.at[0], held_tok.at[1], held_in, held_down)
    moves = []
    for n, (src, held, dst) in enumerate(zip(sources, helds, targets)):
        pieces = PIECES if src.shape[0] % (16 * PIECES) == 0 else 1
        size = src.shape[0] // pieces
        for p in range(pieces):
            at = pl.ds(p * size, size)
            moves.append((pltpu.make_async_copy(src.at[at], held.at[at], in_sem.at[n, p]),
                          pltpu.make_async_copy(held.at[at], dst.at[at], out_sem.at[n, p])))
    for load, _ in moves:
        load.start()
    for load, store in moves:
        load.wait()
        store.start()
    for _, store in moves:
        store.wait()


def shards(tokens_fwd, experts_fwd, scores_fwd, tokens_bwd, experts_bwd, scores_bwd,
           cotangent, w_in, w_down):
    G, inner = lax.axis_size("group"), lax.axis_size("inner")
    n = G * inner
    T, top = experts_fwd.shape
    width = tokens_fwd.shape[1]
    ff = w_down.shape[1]
    capacity = max(2, 3 * T * top // (2 * n))
    C = -(-capacity // 8) * 8
    Z = max(d for d in range(1, inner + 1) if inner % d == 0 and d * d <= n)
    L = inner // Z
    H = math.isqrt(G)
    assert H * H == G
    D = H * L
    rows = n * C
    J = 2
    assert Z % J == 0
    lanes = -(-J * T // 128) * 128
    dma = pltpu.SemaphoreType.DMA
    hbm = pl.BlockSpec(memory_space=pl.ANY)
    tg = math.gcd(tile_of(ff, 256), tile_of(width, 256))
    results = pl.pallas_call(
        functools.partial(layer_kernel, (Z, H, L, C, T, J, inner)),
        out_shape=(
            jax.ShapeDtypeStruct((T, width), BF),
            jax.ShapeDtypeStruct((T, width), BF),
            jax.ShapeDtypeStruct((width, 2 * ff), BF),
            jax.ShapeDtypeStruct((ff, width), BF),
        ),
        in_specs=[hbm] * 9,
        out_specs=(hbm,) * 4,
        scratch_shapes=[
            pltpu.VMEM((2, top, T), jnp.int32), pltpu.VMEM((2, top, T), F32),
            pltpu.VMEM((2, T, width), BF), dma((7,)),
            pltpu.VMEM((H * Z, 4 * D, lanes), F32),
            pltpu.VMEM((H * Z, 4 * D, lanes), F32),
            pltpu.VMEM((width, 2 * ff), BF),
            pltpu.VMEM((ff, width), BF),
            pltpu.VMEM((rows, width), BF),
            pltpu.VMEM((rows, width), BF),
            pltpu.VMEM((rows, width), BF),
            pltpu.VMEM((rows, ff), BF),
            pltpu.VMEM((rows, 2 * ff), BF),
            pltpu.VMEM((3, H * Z, T, width), BF),
            pltpu.VMEM((3, rows, width), BF),
            pltpu.VMEM((2, Z, T, width), BF),
            pltpu.VMEM((2, (H - 1) * Z, T, width), BF),
            pltpu.VMEM((2, (H - 1) * (J - 1), T, width), BF),
            pltpu.VMEM((max(2 * tg, rows // 2), max(2 * ff, width)), BF),
            dma((2,)),
            dma((5, H * Z)), dma((2,)), dma((H, Z)), dma((H, Z)), dma((3, 2, Z)), dma((3, Z)),
            dma((3, H, Z)), dma((3, H, Z)), dma((3, n)), dma((3, n)),
            dma((2, n)), dma((2, n)), dma((2, H, Z)), dma((2, H, Z)), dma((2, Z)), dma((2, Z)),
            dma((3, H, J)), dma((3, H, J)), dma((2, H * J)), dma((2, H * J)),
            pltpu.SemaphoreType.REGULAR((2, Z // J)),
        ],
        compiler_params=pltpu.CompilerParams(
            collective_id=0, has_side_effects=True, vmem_limit_bytes=67043328),
        name="moe_layer",
    )(experts_fwd.T, scores_fwd.T, experts_bwd.T, scores_bwd.T, tokens_bwd, cotangent, tokens_fwd, w_in[0], w_down[0])
    out_fwd, grad_tok, grad_in, grad_down = pl.pallas_call(
        hand_over,
        out_shape=tuple(jax.ShapeDtypeStruct(r.shape, r.dtype) for r in results),
        in_specs=[hbm] * 4,
        out_specs=(hbm,) * 4,
        scratch_shapes=[
            pltpu.VMEM((width, 2 * ff), BF), pltpu.VMEM((ff, width), BF), pltpu.VMEM((2, T, width), BF),
            dma((4, PIECES)), dma((4, PIECES)),
        ],
        compiler_params=pltpu.CompilerParams(vmem_limit_bytes=67043328),
        name="hand_over",
    )(*results)
    return out_fwd, grad_tok, grad_in[None], grad_down[None]


def solution(mesh):
    two, three = P(("group", "inner"), None), P(("group", "inner"), None, None)
    return jax.shard_map(
        shards, mesh=mesh,
        in_specs=(two,) * 7 + (three,) * 2,
        out_specs=(two, two, three, three),
        check_vma=False,
    )
```
